128 devices in a mesh: slab: 16 (over y, z), col: 8 (over x, core).
Axes of the slice: x: 4, y: 4, z: 4, core: 2. Of those that a mesh axis runs over, the one named last changes fastest.
Arguments:
- dist: float32 [19, 256, 64, 1024], P(None, 'slab', None, 'col'), may hold values from 0.6 to 1.4
- fraction: bfloat16 [16, 8, 3, 3, 8, 2, 8, 128], P('slab', 'col'), may hold values from 0 to 0.5
- send_table: int32 [16, 8, 3, 3, 8], P('slab', 'col'), may hold values from -1 to 127, as said below
- recv_table: int32 [16, 8, 3, 3, 8], P('slab', 'col'), may hold values from -1 to 63, as said below
- motion: float32 [9, 256], P(None, ('slab', 'col')), as said below
Outputs:
- dist_next: float32 [19, 256, 64, 1024], P(None, 'slab', None, 'col')
- loads: float32 [6, 256], P(None, ('slab', 'col'))
The draws below stay inside these ranges and needn't reach their ends.
Inputs may be any that keep to these rules, and one draw needn't show every extreme that they name: `send_table`: entry (p, q, a, b, j) is -1 for an empty slot, else s * 64 + k: owned sphere s of device (p, q) covers block k of the device at offset (a - 1, b - 1) along slab and col, taken periodically. Blocks of a device are numbered x-block * 8 + z-block. `recv_table`: entry (p, q, a, b, j) equals send_table[p + a - 1, q + b - 1, 2 - a, 2 - b, j] mod 64 where that entry is live and -1 where it is empty, indices taken periodically. No block of a device is covered by more than two live slots. Some device has all of its 72 incoming slots live. `motion`: rows 0 to 2: sphere centre in cells from the owner's first cell, within [0, 16), [0, 128), [0, 64); rows 3 to 5 velocity; rows 6 to 8 angular velocity.
All inputs are finite; a program needn't handle non-finite values.
Results may differ from the reference program's by a relative error of at most 0.00055.
Values may be sent and summed in bfloat16 or wider, within the bound.
A program may use at most 256 MiB of HBM per device.

```python
import jax
import jax.numpy as jnp
import numpy as np
from jax import lax

CX = 16
CY = 128
NZ = 64
BX = 2
BZ = 8
S_DEV = 2
SLABS = 16
COLS = 8
NX = 256
NY = 1024
NBLK = 64
KD = 8
BC = 2048
SPHERES = 256


def intersection_tables(key):
    key_perm, key_live, key_full, key_sphere = jax.random.split(key, 4)
    devices = SLABS * COLS
    slots = 9 * KD
    perm_keys = jax.random.split(key_perm, devices)
    places = jax.vmap(lambda single: jax.random.permutation(single, 2 * NBLK)[:slots])(perm_keys)
    blocks = (places % NBLK).reshape(SLABS, COLS, 3, 3, KD)
    lowest = KD // 3
    counts = jax.random.randint(key_live, (SLABS, COLS, 3, 3, 1), lowest, KD + 1)
    fullest = jax.random.randint(key_full, (), 0, devices)
    emptiest = (fullest + 1) % devices
    device_ids = jnp.arange(devices).reshape(SLABS, COLS, 1, 1, 1)
    counts = jnp.where(device_ids == fullest, KD, counts)
    counts = jnp.where(device_ids == emptiest, lowest, counts)
    live = jnp.arange(KD).reshape(1, 1, 1, 1, KD) < counts
    spheres = jax.random.randint(key_sphere, (SLABS, COLS, 3, 3, KD), 0, S_DEV)
    received = jnp.where(live, blocks, -1).astype(jnp.int32)
    codes = jnp.where(live, spheres * NBLK + blocks, -1).astype(jnp.int32)
    rows = []
    for slab_pick in range(3):
        row = []
        for col_pick in range(3):
            row.append(jnp.roll(codes[:, :, 2 - slab_pick, 2 - col_pick], (1 - slab_pick, 1 - col_pick), axis=(0, 1)))
        rows.append(jnp.stack(row, axis=2))
    sent = jnp.stack(rows, axis=2).astype(jnp.int32)
    return (sent, received)


def draw_send_table(key, part):
    return intersection_tables(jax.random.fold_in(key, 11))[0]


def draw_recv_table(key, part):
    return intersection_tables(jax.random.fold_in(key, 11))[1]


def draw_motion(key, part):
    key_place, key_move, key_turn = jax.random.split(key, 3)
    uniform_draw = jax.random.uniform(key_place, (3, SPHERES), jnp.float32)
    extent = jnp.array([CX, CY, NZ], jnp.float32).reshape(3, 1)
    centre = uniform_draw * extent * 0.999
    moving = jnp.clip(0.06 * jax.random.normal(key_move, (3, SPHERES), jnp.float32), -0.15, 0.15)
    rotation = jnp.clip(0.03 * jax.random.normal(key_turn, (3, SPHERES), jnp.float32), -0.08, 0.08)
    return jnp.concatenate([centre, moving, rotation], axis=0).astype(jnp.float32)


def steps_of(rng, shape, pieces, least, high):
    def one(dim, shards_of):
        heights = jax.random.uniform(jax.random.fold_in(jax.random.fold_in(rng, 6), dim), (shards_of,), jnp.float32, least / len(pieces), high / len(pieces))
        return jnp.repeat(jnp.exp(heights), shape[dim] // shards_of).reshape((-1,) + (1,) * (len(shape) - dim - 1))

    loudness = one(*pieces[0])
    for cut in pieces[1:]:
        loudness = loudness * one(*cut)
    return loudness


def setup_inputs(seed: int = 0) -> dict:
    key_list = jax.random.split(jax.random.key(seed), 6)
    dist = jnp.clip(0.6 + 0.79999995 * jax.random.uniform(key_list[0], (19, NX, NZ, NY), jnp.float32) ** steps_of(key_list[0], (19, NX, NZ, NY), ((1, 16), (3, 8)), -0.2, 0.2), 0.6, 1.4)
    fraction = jnp.clip(0.5 * jax.random.uniform(key_list[1], (SLABS, COLS, 3, 3, KD, BX, BZ, CY), jnp.float32) ** steps_of(key_list[1], (SLABS, COLS, 3, 3, KD, BX, BZ, CY), ((0, 16), (1, 8)), -0.2, 0.2), 0.0, 0.5).astype(jnp.bfloat16)
    send_table = draw_send_table(jax.random.fold_in(key_list[5], 71), 0)
    recv_table = draw_recv_table(jax.random.fold_in(key_list[5], 71), 0)
    motion = draw_motion(jax.random.fold_in(key_list[5], 71), 0)
    return {"dist": dist, "fraction": fraction, "send_table": send_table, "recv_table": recv_table, "motion": motion}


velocity_table = np.array([[0, 0, 0], [1, 0, 0], [-1, 0, 0], [0, 1, 0], [0, -1, 0], [0, 0, 1], [0, 0, -1], [1, 1, 0], [-1, -1, 0], [1, -1, 0], [-1, 1, 0], [1, 0, 1], [-1, 0, -1], [1, 0, -1], [-1, 0, 1], [0, 1, 1], [0, -1, -1], [0, 1, -1], [0, -1, 1]], dtype=np.float32)
weight_table = np.array([1.0 / 3.0] + [1.0 / 18.0] * 6 + [1.0 / 36.0] * 12, dtype=np.float32)
opposite_index = [0, 2, 1, 4, 3, 6, 5, 8, 7, 10, 9, 12, 11, 14, 13, 16, 15, 18, 17]
relax_time = 0.9
highest = lax.Precision.HIGHEST


def square_table():
    column_x = velocity_table[:, 0]
    column_y = velocity_table[:, 1]
    column_z = velocity_table[:, 2]
    return np.stack([column_x * column_x, column_y * column_y, column_z * column_z, 2.0 * column_x * column_y, 2.0 * column_x * column_z, 2.0 * column_y * column_z], axis=1).astype(np.float32)


def fluid_moments(dist):
    density = jnp.sum(dist, axis=0)
    momentum = jnp.tensordot(jnp.asarray(velocity_table.T), dist, axes=1, precision=highest)
    return density, momentum / density


def weights_like(density):
    return jnp.asarray(weight_table).reshape((19,) + (1,) * density.ndim)


def equilibrium(density, velocity):
    along = jnp.tensordot(jnp.asarray(velocity_table), velocity, axes=1, precision=highest)
    speed_sq = jnp.sum(velocity * velocity, axis=0)
    return weights_like(density) * density * (1.0 + 3.0 * along + 4.5 * along * along - 1.5 * speed_sq)


def collide(dist, density, velocity, totals):
    equil = equilibrium(density, velocity)
    dist_back = jnp.stack([dist[index] for index in opposite_index])
    equil_back = jnp.stack([equil[index] for index in opposite_index])
    bounce = dist_back - equil_back - dist
    solid = totals[0]
    linear = jnp.tensordot(jnp.asarray(velocity_table), totals[1:4], axes=1, precision=highest)
    square = jnp.tensordot(jnp.asarray(square_table()), totals[4:10], axes=1, precision=highest)
    trace_sum = totals[4] + totals[5] + totals[6]
    moving_part = weights_like(density) * density * (solid + 3.0 * linear + 4.5 * square - 1.5 * trace_sum)
    return dist - (1.0 - solid) / relax_time * (dist - equil) + solid * bounce + moving_part


def wall_shift(plane, post, index):
    step_z = int(velocity_table[index, 2])
    back = post[opposite_index[index]]
    if step_z == 1:
        return jnp.concatenate([back[:, 0:1, :], plane[:, :-1, :]], axis=1)
    if step_z == -1:
        return jnp.concatenate([plane[:, 1:, :], back[:, -1:, :]], axis=1)
    return plane


def cell_positions(anchor_x, anchor_y, anchor_z, block_x, block_z, cells_y):
    full_shape = anchor_x.shape + (block_x, block_z, cells_y)
    centre_x = (anchor_x[..., None, None, None] + jnp.arange(block_x).reshape(block_x, 1, 1)).astype(jnp.float32) + 0.5
    centre_y = (anchor_y[..., None, None, None] + jnp.arange(cells_y).reshape(1, 1, cells_y)).astype(jnp.float32) + 0.5
    centre_z = (anchor_z[..., None, None, None] + jnp.arange(block_z).reshape(1, block_z, 1)).astype(jnp.float32) + 0.5
    return jnp.broadcast_to(centre_x, full_shape), jnp.broadcast_to(centre_y, full_shape), jnp.broadcast_to(centre_z, full_shape)


def surface_velocity(params, centre_x, centre_y, centre_z, cells_y):
    def expand(row):
        return params[row][..., None, None, None]
    lever_x = (centre_x - expand(0)) / cells_y
    lever_y = (centre_y - expand(1)) / cells_y
    lever_z = (centre_z - expand(2)) / cells_y
    flow_x = expand(3) + (expand(7) * lever_z - expand(8) * lever_y)
    flow_y = expand(4) + (expand(8) * lever_x - expand(6) * lever_z)
    flow_z = expand(5) + (expand(6) * lever_y - expand(7) * lever_x)
    return jnp.stack([flow_x, flow_y, flow_z], axis=-4), jnp.stack([lever_x, lever_y, lever_z], axis=-4)


def slot_moments(weight, flow):
    along_x = flow[..., 0, :, :, :]
    along_y = flow[..., 1, :, :, :]
    along_z = flow[..., 2, :, :, :]
    return jnp.stack([weight, weight * along_x, weight * along_y, weight * along_z, weight * along_x * along_x, weight * along_y * along_y, weight * along_z * along_z, weight * along_x * along_y, weight * along_x * along_z, weight * along_y * along_z], axis=-4)


def pick_rows(blocks_of, chosen_ids):
    return jnp.take(blocks_of, chosen_ids, axis=0)


def reference(dist, fraction, send_table, recv_table, motion):
    zblocks = NZ // BZ
    xblocks = CX // BX
    density, velocity = fluid_moments(dist)
    frac_rows = []
    code_rows = []
    for slab_pick in range(3):
        frac_row = []
        code_row = []
        for col_pick in range(3):
            frac_row.append(jnp.roll(fraction[:, :, 2 - slab_pick, 2 - col_pick], (1 - slab_pick, 1 - col_pick), axis=(0, 1)))
            code_row.append(jnp.roll(send_table[:, :, 2 - slab_pick, 2 - col_pick], (1 - slab_pick, 1 - col_pick), axis=(0, 1)))
        frac_rows.append(jnp.stack(frac_row, axis=2))
        code_rows.append(jnp.stack(code_row, axis=2))
    frac_view = jnp.stack(frac_rows, axis=2).astype(jnp.float32)
    code_view = jnp.stack(code_rows, axis=2)
    live = recv_table >= 0
    safe = jnp.where(live, recv_table, 0)
    slab_ids = jnp.arange(SLABS).reshape(SLABS, 1, 1, 1, 1)
    col_ids = jnp.arange(COLS).reshape(1, COLS, 1, 1, 1)
    pick_slab = jnp.arange(3).reshape(1, 1, 3, 1, 1)
    pick_col = jnp.arange(3).reshape(1, 1, 1, 3, 1)
    owner = ((slab_ids + pick_slab - 1) % SLABS) * COLS + (col_ids + pick_col - 1) % COLS
    sphere = (owner * S_DEV + jnp.where(code_view >= 0, code_view // NBLK, 0)).astype(jnp.int32)
    params = motion[:, sphere]
    anchor_x = (1 - pick_slab) * CX + (safe // zblocks) * BX
    anchor_y = (1 - pick_col) * CY + jnp.zeros_like(safe)
    anchor_z = (safe % zblocks) * BZ
    centre_x, centre_y, centre_z = cell_positions(anchor_x, anchor_y, anchor_z, BX, BZ, CY)
    flow, lever = surface_velocity(params, centre_x, centre_y, centre_z, CY)
    rounded = lax.optimization_barrier(flow.astype(jnp.bfloat16))
    flow = rounded.astype(jnp.float32)
    gap = relax_time - 0.5
    weight = jnp.where(live[..., None, None, None], frac_view * gap / ((1.0 - frac_view) + gap), 0.0)
    moments = slot_moments(weight, flow)
    device_ids = slab_ids * COLS + col_ids
    targets = (device_ids * NBLK + safe).reshape(-1)
    summed = jax.ops.segment_sum(moments.reshape(targets.shape[0], -1), targets, num_segments=SLABS * COLS * NBLK)
    totals = summed.reshape(SLABS, COLS, xblocks, zblocks, 10, BX, BZ, CY).transpose(4, 0, 2, 5, 3, 6, 1, 7).reshape(10, NX, NZ, NY)
    post = collide(dist, density, velocity, totals)
    planes = []
    for index in range(19):
        step_x = int(velocity_table[index, 0])
        step_y = int(velocity_table[index, 1])
        plane = jnp.roll(post[index], (step_x, step_y), axis=(0, 2))
        planes.append(wall_shift(plane, post, index))
    dist_next = jnp.stack(planes)
    fluid = jnp.concatenate([density[None], velocity], axis=0)
    fluid_view = fluid.reshape(4, SLABS, xblocks, BX, zblocks, BZ, COLS, CY).transpose(1, 6, 2, 4, 0, 3, 5, 7).reshape(SLABS, COLS, NBLK, 4, BX, BZ, CY)
    slot_fluid = jax.vmap(jax.vmap(pick_rows))(fluid_view, safe)
    momentum = weight[..., None, :, :, :] * slot_fluid[..., 0:1, :, :, :] * (flow - slot_fluid[..., 1:4, :, :, :])
    force = -jnp.sum(momentum, axis=(-3, -2, -1)) / BC
    lever_x = lever[..., 0, :, :, :]
    lever_y = lever[..., 1, :, :, :]
    lever_z = lever[..., 2, :, :, :]
    push_x = momentum[..., 0, :, :, :]
    push_y = momentum[..., 1, :, :, :]
    push_z = momentum[..., 2, :, :, :]
    torque = jnp.stack([-jnp.sum(lever_y * push_z - lever_z * push_y, axis=(-3, -2, -1)) / BC, -jnp.sum(lever_z * push_x - lever_x * push_z, axis=(-3, -2, -1)) / BC, -jnp.sum(lever_x * push_y - lever_y * push_x, axis=(-3, -2, -1)) / BC], axis=-1)
    slot_loads = jnp.where(live[..., None], jnp.concatenate([force, torque], axis=-1), 0.0)
    loads = jax.ops.segment_sum(slot_loads.reshape(-1, 6), sphere.reshape(-1), num_segments=SPHERES)
    return dist_next, loads.T
```

```python
import functools

import jax
import jax.numpy as jnp
from jax import lax
from jax.experimental import pallas as pl
from jax.experimental.pallas import tpu as pltpu
from jax.sharding import PartitionSpec as P

F32 = jnp.float32
MESH = pl.DeviceIdType.MESH
TAU = 0.9
GAP = TAU - 0.5

AXIS_PAIRS = [(1, 2, 0), (3, 4, 1), (5, 6, 2)]
PLANE_PAIRS = [(7, 8, 9, 10, 0, 1), (11, 12, 13, 14, 0, 2), (15, 16, 17, 18, 1, 2)]
VEL = [
    (0, 0, 0),
    (1, 0, 0), (-1, 0, 0), (0, 1, 0), (0, -1, 0), (0, 0, 1), (0, 0, -1),
    (1, 1, 0), (-1, -1, 0), (1, -1, 0), (-1, 1, 0),
    (1, 0, 1), (-1, 0, -1), (1, 0, -1), (-1, 0, 1),
    (0, 1, 1), (0, -1, -1), (0, 1, -1), (0, -1, 1),
]
OPP = [0, 2, 1, 4, 3, 6, 5, 8, 7, 10, 9, 12, 11, 14, 13, 16, 15, 18, 17]
KEPT = [1, 7, 9, 11, 13, 2, 8, 10, 12, 14, 0, 3, 4, 5, 6, 15, 16, 17, 18]
SLOT = {pop: place for place, pop in enumerate(KEPT)}
RISING = [3, 7, 10, 15, 17]
FALLING = [4, 8, 9, 16, 18]
CORNERS = [(7, 1, 1), (10, -1, 1), (9, 1, -1), (8, -1, -1)]
OFFSETS = [(a, b) for a in range(3) for b in range(3) if (a, b) != (1, 1)]
N_FIELD = 7


def step_kernel(
    sizes, dist_hbm, frac_hbm, send_ref, recv_ref, motion_ref,
    post_ref, yin_ref, total_ref,
    cells_buf, fluid_buf, frac_in, par_out, par_in, slot_buf, table_v, table_s,
    ypack, corner_out, corner_in, part_out, part_in,
    dist_sem, frac_send, frac_recv, par_send, par_recv, local_sem,
    xr_send, xr_recv, yr_send, yr_recv, cr_send, cr_recv, ld_send, ld_recv,
):
    slabs, cols, nx, nz, ny, kd = sizes
    nbx, nbz = nx // 2, nz // 8
    slots = 9 * kd
    me_p, me_q = lax.axis_index("slab"), lax.axis_index("col")

    def at(dp, dq):
        return (lax.rem(me_p + (dp + slabs), slabs), lax.rem(me_q + (dq + cols), cols))

    def remote(src, dst, send_sem, recv_sem, dp, dq):
        return pltpu.make_async_remote_copy(
            src_ref=src, dst_ref=dst, send_sem=send_sem, recv_sem=recv_sem,
            device_id=at(dp, dq), device_id_type=MESH,
        )

    def row_of(step):
        return lax.rem(nbx - step, nbx)

    def dist_copy(step):
        rows = pl.ds(row_of(step) * 2, 2)
        return pltpu.make_async_copy(
            dist_hbm.at[:, rows], cells_buf.at[:, rows], dist_sem.at[step]
        )

    barrier = pltpu.get_barrier_semaphore()
    for a, b in OFFSETS:
        pl.semaphore_signal(barrier, inc=1, device_id=at(a - 1, b - 1), device_id_type=MESH)

    for step in range(nbx):
        dist_copy(step).start()
    own_copy = pltpu.make_async_copy(frac_hbm.at[0, 0, 1, 1], frac_in.at[4], local_sem.at[0])
    own_copy.start()

    lane = lax.broadcasted_iota(jnp.int32, (8, 128), 1)
    sub = lax.broadcasted_iota(jnp.int32, (8, 128), 0)

    base = jnp.zeros((8, 128), F32)
    for s in range(2):
        for r in range(9):
            base = jnp.where(lane == 9 * s + r, motion_ref[s, r], base)
    for a in range(3):
        for b in range(3):
            row = base
            for j in range(kd):
                second = (send_ref[0, a, b, 0, j] >= nbx * nbz).astype(F32)
                row = jnp.where(lane == 18 + j, second, row)
            if (a, b) == (1, 1):
                par_in[4] = row
            else:
                par_out[a * 3 + b] = row

    pl.semaphore_wait(barrier, len(OFFSETS))
    payload = {}
    for a, b in OFFSETS:
        out, land = a * 3 + b, (2 - a) * 3 + (2 - b)
        payload[land] = (
            remote(frac_hbm.at[0, 0, a, b], frac_in.at[land],
                   frac_send.at[out], frac_recv.at[land], a - 1, b - 1),
            remote(par_out.at[out], par_in.at[land],
                   par_send.at[out], par_recv.at[land], a - 1, b - 1),
        )
        for copy in payload[land]:
            copy.start()

    first = jnp.full((8, 128), slots, jnp.int32)
    other = jnp.full((8, 128), slots, jnp.int32)
    for n in range(9):
        for j in range(kd):
            hit = lane == recv_ref[0, n // 3, n % 3, 0, j]
            free = first == slots
            other = jnp.where(hit & jnp.logical_not(free), n * kd + j, other)
            first = jnp.where(hit & free, n * kd + j, first)
    table_v[0] = first
    table_v[1] = other
    table_copy = pltpu.make_async_copy(table_v, table_s, local_sem.at[1])
    table_copy.start()
    for c in range(N_FIELD):
        slot_buf[slots, c] = jnp.zeros((8, 128), F32)
    ypack[...] = jnp.zeros_like(ypack)

    def moments_row(step, _):
        dist_copy(step).wait()
        bx = row_of(step)

        def moments_block(bz, _):
            rows = pl.ds(pl.multiple_of(bz * 8, 8), 8)
            for dx in range(2):
                x = bx * 2 + dx
                plus, minus = {}, {}
                for i in range(1, 19, 2):
                    ahead = cells_buf[i, x, rows, :]
                    back = cells_buf[i + 1, x, rows, :]
                    plus[i] = ahead + back
                    minus[i] = ahead - back
                    cells_buf[i, x, rows, :] = plus[i]
                    cells_buf[i + 1, x, rows, :] = minus[i]
                density = cells_buf[0, x, rows, :]
                for i in range(1, 19, 2):
                    density = density + plus[i]
                inverse = 1.0 / density
                mom_x = (minus[1] + (minus[7] + minus[9])) + (minus[11] + minus[13])
                mom_y = (minus[3] + (minus[7] - minus[9])) + (minus[15] + minus[17])
                mom_z = (minus[5] + (minus[11] - minus[13])) + (minus[15] - minus[17])
                block = bx * nbz + bz
                fluid_buf[block, 0, dx] = density
                fluid_buf[block, 1, dx] = mom_x * inverse
                fluid_buf[block, 2, dx] = mom_y * inverse
                fluid_buf[block, 3, dx] = mom_z * inverse
            return 0

        return lax.fori_loop(0, nbz, moments_block, 0)

    lax.fori_loop(0, nbx, moments_row, 0)

    own_copy.wait()
    for pair in payload.values():
        for copy in pair:
            copy.wait_recv()

    pos_y = lane.astype(F32) + 0.5
    pos_z = sub.astype(F32) + 0.5

    def slot_place(n, j):
        block = recv_ref[0, n // 3, n % 3, 0, j]
        return block >= 0, jnp.maximum(block, 0)

    def spread(row, place):
        return jnp.broadcast_to(row[:, place:place + 1], (8, 128))

    def slot_sphere(row, j, both):
        second = spread(row, 18 + j) > 0.5
        return second, [jnp.where(second, both[9 + r], both[r]) for r in range(len(both) - 9)]

    def levers(n, safe, centre):
        a, b = n // 3, n % 3
        from_x = ((1 - a) * nx + lax.div(safe, nbz) * 2).astype(F32)
        from_y = ((1 - b) * ny).astype(F32)
        from_z = (lax.rem(safe, nbz) * 8).astype(F32)
        scale = 1.0 / ny
        lever_x = [((from_x + (dx + 0.5)) - centre[0]) * scale for dx in range(2)]
        lever_y = ((pos_y + from_y) - centre[1]) * scale
        lever_z = ((pos_z + from_z) - centre[2]) * scale
        return lever_x, lever_y, lever_z

    def rounded(value):
        return value.astype(jnp.bfloat16).astype(F32)

    def slots_of(n, _):
        row = par_in[n]
        both = [spread(row, r) for r in range(18)]
        for j in range(kd):
            live, safe = slot_place(n, j)
            _, prm = slot_sphere(row, j, both)
            lever_x, lever_y, lever_z = levers(n, safe, prm)
            vx, vy, vz, wx, wy, wz = prm[3:9]
            slot = n * kd + j
            slot_buf[slot, 2] = rounded(vx + (wy * lever_z - wz * lever_y))
            for dx in range(2):
                frac = frac_in[n, j, dx].astype(F32)
                weight = frac * GAP / ((1.0 - frac) + GAP)
                slot_buf[slot, dx] = jnp.where(live, weight, 0.0)
                slot_buf[slot, 3 + dx] = rounded(vy + (wz * lever_x[dx] - wx * lever_z))
                slot_buf[slot, 5 + dx] = rounded(vz + (wx * lever_y - wy * lever_x[dx]))
        return 0

    lax.fori_loop(0, 9, slots_of, 0)
    table_copy.wait()

    def collide_block(bx, bz):
        rows = pl.ds(pl.multiple_of(bz * 8, 8), 8)
        block = bx * nbz + bz
        one, two = table_s[0, 0, block], table_s[1, 0, block]
        up, down = jnp.zeros((8, 128), F32), jnp.zeros((8, 128), F32)
        for dx in range(2):
            x = bx * 2 + dx
            fields = []
            for slot in (one, two):
                weight = slot_buf[slot, dx]
                flow = [slot_buf[slot, 2], slot_buf[slot, 3 + dx], slot_buf[slot, 5 + dx]]
                first_m = [weight * f for f in flow]
                second_m = [
                    first_m[0] * flow[0], first_m[1] * flow[1], first_m[2] * flow[2],
                    first_m[0] * flow[1], first_m[0] * flow[2], first_m[1] * flow[2],
                ]
                fields.append([weight] + first_m + second_m)
            total = [u + v for u, v in zip(*fields)]
            solid = total[0]
            density = fluid_buf[block, 0, dx]
            vel = [fluid_buf[block, 1 + c, dx] for c in range(3)]
            relax = (1.0 - solid) * (1.0 / TAU)
            keep = 0.5 - 0.5 * relax
            keep_odd = keep - solid
            even_rho = (relax - solid) * density
            odd_rho = (relax + solid) * density
            scaled = [even_rho * v for v in vel]
            flux = [odd_rho * vel[c] + density * total[1 + c] for c in range(3)]
            t_xx = scaled[0] * vel[0] + density * total[4]
            t_yy = scaled[1] * vel[1] + density * total[5]
            t_zz = scaled[2] * vel[2] + density * total[6]
            t_xy = scaled[0] * vel[1] + density * total[7]
            t_xz = scaled[0] * vel[2] + density * total[8]
            t_yz = scaled[1] * vel[2] + density * total[9]
            rest = relax * density - 1.5 * ((t_xx + t_yy) + t_zz)
            outs = {0: (keep + keep) * cells_buf[0, x, rows, :] + (1.0 / 3.0) * rest}
            rest_axis = (1.0 / 18.0) * rest
            rest_plane = (1.0 / 36.0) * rest
            diag = [t_xx, t_yy, t_zz]
            for i, back, c in AXIS_PAIRS:
                even = keep * cells_buf[i, x, rows, :] + (rest_axis + 0.25 * diag[c])
                odd = keep_odd * cells_buf[i + 1, x, rows, :] + (1.0 / 6.0) * flux[c]
                outs[i] = even + odd
                outs[back] = even - odd
            eighth = [0.125 * d for d in diag]
            twelfth = [(1.0 / 12.0) * f for f in flux]
            cross = {(0, 1): t_xy, (0, 2): t_xz, (1, 2): t_yz}
            for i, i_back, j, j_back, c, d in PLANE_PAIRS:
                middle = rest_plane + (eighth[c] + eighth[d])
                tilt = 0.25 * cross[(c, d)]
                even = keep * cells_buf[i, x, rows, :] + (middle + tilt)
                odd = keep_odd * cells_buf[i + 1, x, rows, :] + (twelfth[c] + twelfth[d])
                outs[i] = even + odd
                outs[i_back] = even - odd
                even = keep * cells_buf[j, x, rows, :] + (middle - tilt)
                odd = keep_odd * cells_buf[j + 1, x, rows, :] + (twelfth[c] - twelfth[d])
                outs[j] = even + odd
                outs[j_back] = even - odd
            for m in range(5):
                place = dx * 5 + m
                rise, fall = outs[RISING[m]], outs[FALLING[m]]
                up = jnp.where(lane == place, pltpu.roll(rise, 1 + place, 1), up)
                down = jnp.where(
                    lane == place, fall if place == 0 else pltpu.roll(fall, place, 1), down
                )
                outs[RISING[m]] = pltpu.roll(rise, 1, 1)
                outs[FALLING[m]] = pltpu.roll(fall, 127, 1)
            for pop in range(19):
                post_ref[SLOT[pop], x + 1, rows, :] = outs[pop]
        start = (2 * bx + 1) * 5
        mine = (lane >= start) & (lane < start + 10)
        ypack[0, rows, :] = jnp.where(mine, pltpu.roll(up, start, 1), ypack[0, rows, :])
        ypack[1, rows, :] = jnp.where(mine, pltpu.roll(down, start, 1), ypack[1, rows, :])

    def collide_row(step, _):
        bx = row_of(step)

        def body(bz, _):
            collide_block(bx, bz)
            return 0

        return lax.fori_loop(0, nbz, body, 0)

    lax.fori_loop(0, 2, collide_row, 0)

    x_copies = [
        remote(post_ref.at[pl.ds(0, 5), nx], post_ref.at[pl.ds(0, 5), 0],
               xr_send.at[0], xr_recv.at[0], 1, 0),
        remote(post_ref.at[pl.ds(5, 5), 1], post_ref.at[pl.ds(5, 5), nx + 1],
               xr_send.at[1], xr_recv.at[1], -1, 0),
    ]
    for copy in x_copies:
        copy.start()
    corner_copies = []
    for n, (pop, sx, sy) in enumerate(CORNERS):
        line = jnp.zeros((8, 128), F32)
        edge = 0 if sy == 1 else 127
        for bz in range(nbz):
            part = post_ref[SLOT[pop], nx if sx == 1 else 1, pl.ds(bz * 8, 8), :]
            shift = (bz - edge) % 128
            line = jnp.where(lane == bz, part if shift == 0 else pltpu.roll(part, shift, 1), line)
        corner_out[n] = line
        copy = remote(corner_out.at[n], corner_in.at[n], cr_send.at[n], cr_recv.at[n], sx, sy)
        copy.start()
        corner_copies.append(copy)

    lax.fori_loop(2, nbx, collide_row, 0)

    y_copies = [
        remote(ypack.at[0], yin_ref.at[0], yr_send.at[0], yr_recv.at[0], 0, 1),
        remote(ypack.at[1], yin_ref.at[1], yr_send.at[1], yr_recv.at[1], 0, -1),
    ]
    for copy in y_copies:
        copy.start()

    def loads_of(n, _):
        row = par_in[n]
        both = [spread(row, 9 * s + r) for s in range(2) for r in range(3)]
        acc = [jnp.zeros((8, 128), F32) for _ in range(12)]
        for j in range(kd):
            _, safe = slot_place(n, j)
            second = spread(row, 18 + j) > 0.5
            centre = [jnp.where(second, both[3 + r], both[r]) for r in range(3)]
            lever_x, lever_y, lever_z = levers(n, safe, centre)
            slot = n * kd + j
            push, turn_y, turn_z = [], 0.0, 0.0
            for dx in range(2):
                wr = slot_buf[slot, dx] * fluid_buf[safe, 0, dx]
                px = wr * (slot_buf[slot, 2] - fluid_buf[safe, 1, dx])
                py = wr * (slot_buf[slot, 3 + dx] - fluid_buf[safe, 2, dx])
                pz = wr * (slot_buf[slot, 5 + dx] - fluid_buf[safe, 3, dx])
                push.append((px, py, pz))
                turn_y = turn_y - lever_x[dx] * pz
                turn_z = turn_z + lever_x[dx] * py
            px, py, pz = [u + v for u, v in zip(*push)]
            values = [
                px, py, pz,
                lever_y * pz - lever_z * py,
                turn_y + lever_z * px,
                turn_z - lever_y * px,
            ]
            for c, value in enumerate(values):
                acc[c] = acc[c] + jnp.where(second, 0.0, value)
                acc[6 + c] = acc[6 + c] + jnp.where(second, value, 0.0)
        for s in range(2):
            stack = jnp.zeros((8, 128), F32)
            for c in range(6):
                total = jnp.sum(acc[6 * s + c], axis=0, keepdims=True)
                stack = jnp.where(sub == c, total, stack)
            part_out[n, pl.ds(8 * s, 8), :] = stack
        return 0

    lax.fori_loop(0, 9, loads_of, 0)
    load_copies = []
    for a, b in OFFSETS:
        out, land = a * 3 + b, (2 - a) * 3 + (2 - b)
        copy = remote(part_out.at[out], part_in.at[land],
                      ld_send.at[out], ld_recv.at[land], a - 1, b - 1)
        copy.start()
        load_copies.append((land, copy))
    total = part_out[4]
    for land, copy in load_copies:
        copy.wait_recv()
        total = total + part_in[land]
    total_ref[...] = total

    for copy in corner_copies + y_copies + x_copies:
        copy.wait_recv()
    for n, (pop, sx, sy) in enumerate(CORNERS):
        way = 0 if sy == 1 else 1
        place = (RISING if sy == 1 else FALLING).index(pop) + (0 if sx == 1 else (nx + 1) * 5)
        line = corner_in[n]
        for bz in range(nbz):
            rows = pl.ds(bz * 8, 8)
            moved = pltpu.roll(line, (place - bz) % 128, 1)
            yin_ref[way, rows, :] = jnp.where(lane == place, moved, yin_ref[way, rows, :])

    for pair in payload.values():
        for copy in pair:
            copy.wait_send()
    for copy in x_copies + corner_copies + y_copies:
        copy.wait_send()
    for _, copy in load_copies:
        copy.wait_send()


def stream_kernel(nz, ny, post_ref, yin_ref, total_ref, out_ref, loads_ref):
    step = pl.program_id(0)
    @pl.when(step == 0)
    def _():
        total = jnp.sum(total_ref[...], axis=1, keepdims=True) * (-1.0 / (2 * 8 * ny))
        place_s = lax.broadcasted_iota(jnp.int32, (2, 6), 0)
        place_c = lax.broadcasted_iota(jnp.int32, (2, 6), 1)
        result = jnp.zeros((2, 6), F32)
        for s in range(2):
            for c in range(6):
                value = jnp.broadcast_to(total[8 * s + c:8 * s + c + 1], (2, 6))
                result = jnp.where((place_s == s) & (place_c == c), value, result)
        loads_ref[...] = result

    lane = lax.broadcasted_iota(jnp.int32, (nz, ny), 1)
    row = lax.broadcasted_iota(jnp.int32, (nz, ny), 0)
    up, down = yin_ref[0], yin_ref[1]
    for dx in range(2):
        x = step * 2 + dx
        for pop in range(19):
            cx, cy, cz = VEL[pop]
            plane = post_ref[SLOT[pop], x + 1 - cx]
            if cy == 1:
                place = (x + 1 - cx) * 5 + RISING.index(pop)
                plane = jnp.where(lane == 0, pltpu.roll(up, 128 - place, 1), plane)
            elif cy == -1:
                place = (x + 1 - cx) * 5 + FALLING.index(pop)
                plane = jnp.where(lane == 127, pltpu.roll(down, 127 - place, 1), plane)
            if cz != 0:
                back = post_ref[SLOT[OPP[pop]], x + 1]
                if cy != 0:
                    back = pltpu.roll(back, 1 if cy == 1 else 127, 1)
                plane = jnp.where(
                    row == (0 if cz == 1 else nz - 1), back,
                    pltpu.roll(plane, 1 if cz == 1 else nz - 1, 0),
                )
            out_ref[pop, dx] = plane


def per_device(mesh_sizes, dist, fraction, send_table, recv_table, motion):
    slabs, cols = mesh_sizes
    nx, nz, ny = dist.shape[1:]
    kd = fraction.shape[4]
    slots = 9 * kd
    blocks = (nx // 2) * (nz // 8)
    hbm = pl.BlockSpec(memory_space=pltpu.HBM)
    smem = pl.BlockSpec(memory_space=pltpu.SMEM)
    vmem = pl.BlockSpec(memory_space=pltpu.VMEM)
    dma = pltpu.SemaphoreType.DMA
    post, yin, total = pl.pallas_call(
        functools.partial(step_kernel, (slabs, cols, nx, nz, ny, kd)),
        out_shape=[
            pltpu.VMEM((19, nx + 2, nz, ny), F32),
            pltpu.VMEM((2, nz, ny), F32),
            pltpu.VMEM((16, 128), F32),
        ],
        in_specs=[hbm, hbm, smem, smem, smem],
        out_specs=[vmem, vmem, vmem],
        scratch_shapes=[
            pltpu.VMEM((19, nx, nz, ny), F32),
            pltpu.VMEM((blocks, 4, 2, 8, ny), F32),
            pltpu.VMEM((9, kd, 2, 8, ny), jnp.bfloat16),
            pltpu.VMEM((9, 8, 128), F32),
            pltpu.VMEM((9, 8, 128), F32),
            pltpu.VMEM((slots + 1, N_FIELD, 8, ny), F32),
            pltpu.VMEM((2, 8, 128), jnp.int32),
            pltpu.SMEM((2, 8, 128), jnp.int32),
            pltpu.VMEM((2, nz, ny), F32),
            pltpu.VMEM((4, 8, 128), F32),
            pltpu.VMEM((4, 8, 128), F32),
            pltpu.VMEM((9, 16, 128), F32),
            pltpu.VMEM((9, 16, 128), F32),
            dma((nx // 2,)), dma((9,)), dma((9,)), dma((9,)), dma((9,)), dma((2,)),
            dma((2,)), dma((2,)), dma((2,)), dma((2,)), dma((4,)), dma((4,)),
            dma((9,)), dma((9,)),
        ],
        compiler_params=pltpu.CompilerParams(
            collective_id=0, has_side_effects=True, vmem_limit_bytes=44 << 20
        ),
        name="collide_exchange",
    )(dist, fraction, *(jnp.transpose(t, (0, 2, 3, 1, 4)) for t in (send_table, recv_table)), motion.T)
    dist_next, loads = pl.pallas_call(
        functools.partial(stream_kernel, nz, ny),
        grid=(nx // 2,),
        out_shape=[jax.ShapeDtypeStruct(dist.shape, F32), jax.ShapeDtypeStruct((2, 6), F32)],
        in_specs=[vmem, vmem, vmem],
        out_specs=[
            pl.BlockSpec((19, 2, nz, ny), lambda step: (0, step, 0, 0)),
            pl.BlockSpec((2, 6), lambda step: (0, 0)),
        ],
        compiler_params=pltpu.CompilerParams(vmem_limit_bytes=8 << 20),
        name="stream",
    )(post, yin, total)
    return (dist_next, loads.T)


def solution(mesh):
    placed = (
        P(None, "slab", None, "col"),
        P("slab", "col", None, None, None, None, None, None),
        P("slab", "col", None, None, None),
        P("slab", "col", None, None, None),
        P(None, ("slab", "col")),
    )
    return jax.shard_map(
        functools.partial(per_device, (mesh.shape["slab"], mesh.shape["col"])),
        mesh=mesh,
        in_specs=placed,
        out_specs=(P(None, "slab", None, "col"), P(None, ("slab", "col"))),
        check_vma=False,
    )
```

```python
import functools

import jax
import jax.numpy as jnp
from jax import lax
from jax.experimental import pallas as pl
from jax.experimental.pallas import tpu as pltpu
from jax.sharding import PartitionSpec as P

F32 = jnp.float32
MESH = pl.DeviceIdType.MESH
TAU = 0.9
GAP = TAU - 0.5

AXIS_PAIRS = [(1, 2, 0), (3, 4, 1), (5, 6, 2)]
PLANE_PAIRS = [(7, 8, 9, 10, 0, 1), (11, 12, 13, 14, 0, 2), (15, 16, 17, 18, 1, 2)]
VEL = [
    (0, 0, 0),
    (1, 0, 0), (-1, 0, 0), (0, 1, 0), (0, -1, 0), (0, 0, 1), (0, 0, -1),
    (1, 1, 0), (-1, -1, 0), (1, -1, 0), (-1, 1, 0),
    (1, 0, 1), (-1, 0, -1), (1, 0, -1), (-1, 0, 1),
    (0, 1, 1), (0, -1, -1), (0, 1, -1), (0, -1, 1),
]
OPP = [0, 2, 1, 4, 3, 6, 5, 8, 7, 10, 9, 12, 11, 14, 13, 16, 15, 18, 17]
KEPT = [1, 7, 9, 11, 13, 2, 8, 10, 12, 14, 0, 3, 4, 5, 6, 15, 16, 17, 18]
SLOT = {pop: place for place, pop in enumerate(KEPT)}
RISING = [3, 7, 10, 15, 17]
FALLING = [4, 8, 9, 16, 18]
CORNERS = [(7, 1, 1), (10, -1, 1), (9, 1, -1), (8, -1, -1)]
OFFSETS = [(a, b) for a in range(3) for b in range(3) if (a, b) != (1, 1)]
N_FIELD = 7


def step_kernel(
    sizes, dist_hbm, frac_hbm, send_ref, recv_ref, motion_ref,
    post_ref, yin_ref, total_ref,
    cells_buf, fluid_buf, frac_in, par_out, par_in, slot_buf, table_v, table_s,
    ypack, corner_out, corner_in, part_out, part_in,
    dist_sem, frac_send, frac_recv, par_send, par_recv, local_sem,
    xr_send, xr_recv, yr_send, yr_recv, cr_send, cr_recv, ld_send, ld_recv,
):
    slabs, cols, nx, nz, ny, kd = sizes
    nbx, nbz = nx // 2, nz // 8
    slots = 9 * kd
    me_p, me_q = lax.axis_index("slab"), lax.axis_index("col")

    def at(dp, dq):
        return (lax.rem(me_p + (dp + slabs), slabs), lax.rem(me_q + (dq + cols), cols))

    def remote(src, dst, send_sem, recv_sem, dp, dq):
        return pltpu.make_async_remote_copy(
            src_ref=src, dst_ref=dst, send_sem=send_sem, recv_sem=recv_sem,
            device_id=at(dp, dq), device_id_type=MESH,
        )

    def row_of(step):
        return lax.rem(nbx - step, nbx)

    def dist_copy(step):
        rows = pl.ds(row_of(step) * 2, 2)
        return pltpu.make_async_copy(
            dist_hbm.at[:, rows], cells_buf.at[:, rows], dist_sem.at[step]
        )

    barrier = pltpu.get_barrier_semaphore()
    for a, b in OFFSETS:
        pl.semaphore_signal(barrier, inc=1, device_id=at(a - 1, b - 1), device_id_type=MESH)

    for step in range(nbx):
        dist_copy(step).start()
    own_copy = pltpu.make_async_copy(frac_hbm.at[0, 0, 1, 1], frac_in.at[4], local_sem.at[0])
    own_copy.start()

    lane = lax.broadcasted_iota(jnp.int32, (8, 128), 1)
    sub = lax.broadcasted_iota(jnp.int32, (8, 128), 0)

    base = jnp.zeros((8, 128), F32)
    for s in range(2):
        for r in range(9):
            base = jnp.where(lane == 9 * s + r, motion_ref[s, r], base)
    for a in range(3):
        for b in range(3):
            row = base
            for j in range(kd):
                second = (send_ref[0, a, b, 0, j] >= nbx * nbz).astype(F32)
                row = jnp.where(lane == 18 + j, second, row)
            if (a, b) == (1, 1):
                par_in[4] = row
            else:
                par_out[a * 3 + b] = row

    pl.semaphore_wait(barrier, len(OFFSETS))
    payload = {}
    for a, b in OFFSETS:
        out, land = a * 3 + b, (2 - a) * 3 + (2 - b)
        payload[land] = (
            remote(frac_hbm.at[0, 0, a, b], frac_in.at[land],
                   frac_send.at[out], frac_recv.at[land], a - 1, b - 1),
            remote(par_out.at[out], par_in.at[land],
                   par_send.at[out], par_recv.at[land], a - 1, b - 1),
        )
        for copy in payload[land]:
            copy.start()

    first = jnp.full((8, 128), slots, jnp.int32)
    other = jnp.full((8, 128), slots, jnp.int32)
    for n in range(9):
        for j in range(kd):
            hit = lane == recv_ref[0, n // 3, n % 3, 0, j]
            free = first == slots
            other = jnp.where(hit & jnp.logical_not(free), n * kd + j, other)
            first = jnp.where(hit & free, n * kd + j, first)
    table_v[0] = first
    table_v[1] = other
    table_copy = pltpu.make_async_copy(table_v, table_s, local_sem.at[1])
    table_copy.start()
    for c in range(N_FIELD):
        slot_buf[slots, c] = jnp.zeros((8, 128), F32)
    ypack[...] = jnp.zeros_like(ypack)

    def moments_row(step, _):
        dist_copy(step).wait()
        bx = row_of(step)

        def moments_block(bz, _):
            rows = pl.ds(pl.multiple_of(bz * 8, 8), 8)
            for dx in range(2):
                x = bx * 2 + dx
                plus, minus = {}, {}
                for i in range(1, 19, 2):
                    ahead = cells_buf[i, x, rows, :]
                    back = cells_buf[i + 1, x, rows, :]
                    plus[i] = ahead + back
                    minus[i] = ahead - back
                    cells_buf[i, x, rows, :] = plus[i]
                    cells_buf[i + 1, x, rows, :] = minus[i]
                density = cells_buf[0, x, rows, :]
                for i in range(1, 19, 2):
                    density = density + plus[i]
                inverse = 1.0 / density
                mom_x = (minus[1] + (minus[7] + minus[9])) + (minus[11] + minus[13])
                mom_y = (minus[3] + (minus[7] - minus[9])) + (minus[15] + minus[17])
                mom_z = (minus[5] + (minus[11] - minus[13])) + (minus[15] - minus[17])
                block = bx * nbz + bz
                fluid_buf[block, 0, dx] = density
                fluid_buf[block, 1, dx] = mom_x * inverse
                fluid_buf[block, 2, dx] = mom_y * inverse
                fluid_buf[block, 3, dx] = mom_z * inverse
            return 0

        return lax.fori_loop(0, nbz, moments_block, 0)

    lax.fori_loop(0, nbx, moments_row, 0)

    pos_y = lane.astype(F32) + 0.5
    pos_z = sub.astype(F32) + 0.5

    def slot_place(n, j):
        block = recv_ref[0, n // 3, n % 3, 0, j]
        return block >= 0, jnp.maximum(block, 0)

    def spread(row, place):
        return jnp.broadcast_to(row[:, place:place + 1], (8, 128))

    def slot_sphere(row, j, both):
        second = spread(row, 18 + j) > 0.5
        return second, [jnp.where(second, both[9 + r], both[r]) for r in range(len(both) - 9)]

    def levers(n, safe, centre):
        a, b = n // 3, n % 3
        from_x = ((1 - a) * nx + lax.div(safe, nbz) * 2).astype(F32)
        from_y = ((1 - b) * ny).astype(F32)
        from_z = (lax.rem(safe, nbz) * 8).astype(F32)
        scale = 1.0 / ny
        lever_x = [((from_x + (dx + 0.5)) - centre[0]) * scale for dx in range(2)]
        lever_y = ((pos_y + from_y) - centre[1]) * scale
        lever_z = ((pos_z + from_z) - centre[2]) * scale
        return lever_x, lever_y, lever_z

    def rounded(value):
        return value.astype(jnp.bfloat16).astype(F32)

    def slots_of(step, _):
        n = lax.rem(step + 3, 9)

        @pl.when(step == 0)
        def _():
            own_copy.wait()

        for group in range(3):
            @pl.when(step == 3 * group)
            def _():
                for land in range(3 * ((group + 1) % 3), 3 * ((group + 1) % 3) + 3):
                    for copy in payload.get(land, ()):
                        copy.wait_recv()

        row = par_in[n]
        both = [spread(row, r) for r in range(18)]
        for j in range(kd):
            live, safe = slot_place(n, j)
            _, prm = slot_sphere(row, j, both)
            lever_x, lever_y, lever_z = levers(n, safe, prm)
            vx, vy, vz, wx, wy, wz = prm[3:9]
            slot = n * kd + j
            slot_buf[slot, 2] = rounded(vx + (wy * lever_z - wz * lever_y))
            for dx in range(2):
                frac = frac_in[n, j, dx].astype(F32)
                weight = frac * GAP / ((1.0 - frac) + GAP)
                slot_buf[slot, dx] = jnp.where(live, weight, 0.0)
                slot_buf[slot, 3 + dx] = rounded(vy + (wz * lever_x[dx] - wx * lever_z))
                slot_buf[slot, 5 + dx] = rounded(vz + (wx * lever_y - wy * lever_x[dx]))
        return 0

    lax.fori_loop(0, 9, slots_of, 0)
    table_copy.wait()

    def collide_block(bx, bz):
        rows = pl.ds(pl.multiple_of(bz * 8, 8), 8)
        block = bx * nbz + bz
        one, two = table_s[0, 0, block], table_s[1, 0, block]
        for dx in range(2):
            x = bx * 2 + dx
            fields = []
            for slot in (one, two):
                weight = slot_buf[slot, dx]
                flow = [slot_buf[slot, 2], slot_buf[slot, 3 + dx], slot_buf[slot, 5 + dx]]
                first_m = [weight * f for f in flow]
                second_m = [
                    first_m[0] * flow[0], first_m[1] * flow[1], first_m[2] * flow[2],
                    first_m[0] * flow[1], first_m[0] * flow[2], first_m[1] * flow[2],
                ]
                fields.append([weight] + first_m + second_m)
            total = [u + v for u, v in zip(*fields)]
            solid = total[0]
            density = fluid_buf[block, 0, dx]
            vel = [fluid_buf[block, 1 + c, dx] for c in range(3)]
            relax = (1.0 - solid) * (1.0 / TAU)
            keep = 0.5 - 0.5 * relax
            keep_odd = keep - solid
            even_rho = (relax - solid) * density
            odd_rho = (relax + solid) * density
            scaled = [even_rho * v for v in vel]
            flux = [odd_rho * vel[c] + density * total[1 + c] for c in range(3)]
            t_xx = scaled[0] * vel[0] + density * total[4]
            t_yy = scaled[1] * vel[1] + density * total[5]
            t_zz = scaled[2] * vel[2] + density * total[6]
            t_xy = scaled[0] * vel[1] + density * total[7]
            t_xz = scaled[0] * vel[2] + density * total[8]
            t_yz = scaled[1] * vel[2] + density * total[9]
            rest = relax * density - 1.5 * ((t_xx + t_yy) + t_zz)
            outs = {0: (keep + keep) * cells_buf[0, x, rows, :] + (1.0 / 3.0) * rest}
            rest_axis = (1.0 / 18.0) * rest
            rest_plane = (1.0 / 36.0) * rest
            diag = [t_xx, t_yy, t_zz]
            for i, back, c in AXIS_PAIRS:
                even = keep * cells_buf[i, x, rows, :] + (rest_axis + 0.25 * diag[c])
                odd = keep_odd * cells_buf[i + 1, x, rows, :] + (1.0 / 6.0) * flux[c]
                outs[i] = even + odd
                outs[back] = even - odd
            eighth = [0.125 * d for d in diag]
            twelfth = [(1.0 / 12.0) * f for f in flux]
            cross = {(0, 1): t_xy, (0, 2): t_xz, (1, 2): t_yz}
            for i, i_back, j, j_back, c, d in PLANE_PAIRS:
                middle = rest_plane + (eighth[c] + eighth[d])
                tilt = 0.25 * cross[(c, d)]
                even = keep * cells_buf[i, x, rows, :] + (middle + tilt)
                odd = keep_odd * cells_buf[i + 1, x, rows, :] + (twelfth[c] + twelfth[d])
                outs[i] = even + odd
                outs[i_back] = even - odd
                even = keep * cells_buf[j, x, rows, :] + (middle - tilt)
                odd = keep_odd * cells_buf[j + 1, x, rows, :] + (twelfth[c] - twelfth[d])
                outs[j] = even + odd
                outs[j_back] = even - odd
            for pop in range(19):
                post_ref[SLOT[pop], x + 1, rows, :] = outs[pop]

    lane_z = lax.broadcasted_iota(jnp.int32, (nz, 128), 1)

    def pack_row(bx):
        start = (2 * bx + 1) * 5
        mine = (lane_z >= start) & (lane_z < start + 10)
        for way, (pops, edge) in enumerate(((RISING, 127), (FALLING, 0))):
            packed = jnp.zeros((nz, 128), F32)
            for dx in range(2):
                for m in range(5):
                    plane = post_ref[SLOT[pops[m]], bx * 2 + dx + 1]
                    place = dx * 5 + m
                    shift = (place - edge) % 128
                    packed = jnp.where(
                        lane_z == place, plane if shift == 0 else pltpu.roll(plane, shift, 1), packed
                    )
            ypack[way] = jnp.where(mine, pltpu.roll(packed, start, 1), ypack[way])

    def collide_row(step, _):
        bx = row_of(step)

        def body(bz, _):
            collide_block(bx, bz)
            return 0

        lax.fori_loop(0, nbz, body, 0)

        @pl.when(step == 0)
        def _():
            x_copies[1].start()

        @pl.when(step == 1)
        def _():
            x_copies[0].start()

        pack_row(bx)
        return 0

    x_copies = [
        remote(post_ref.at[pl.ds(0, 5), nx], post_ref.at[pl.ds(0, 5), 0],
               xr_send.at[0], xr_recv.at[0], 1, 0),
        remote(post_ref.at[pl.ds(5, 5), 1], post_ref.at[pl.ds(5, 5), nx + 1],
               xr_send.at[1], xr_recv.at[1], -1, 0),
    ]
    lax.fori_loop(0, 2, collide_row, 0)

    corner_copies = []
    for n, (pop, sx, sy) in enumerate(CORNERS):
        line = jnp.zeros((8, 128), F32)
        edge = 127 if sy == 1 else 0
        for bz in range(nbz):
            part = post_ref[SLOT[pop], nx if sx == 1 else 1, pl.ds(bz * 8, 8), :]
            shift = (bz - edge) % 128
            line = jnp.where(lane == bz, part if shift == 0 else pltpu.roll(part, shift, 1), line)
        corner_out[n] = line
        copy = remote(corner_out.at[n], corner_in.at[n], cr_send.at[n], cr_recv.at[n], sx, sy)
        copy.start()
        corner_copies.append(copy)

    def loads_of(n, _):
        row = par_in[n]
        both = [spread(row, 9 * s + r) for s in range(2) for r in range(3)]
        acc = [jnp.zeros((8, 128), F32) for _ in range(12)]
        for j in range(kd):
            _, safe = slot_place(n, j)
            second = spread(row, 18 + j) > 0.5
            centre = [jnp.where(second, both[3 + r], both[r]) for r in range(3)]
            lever_x, lever_y, lever_z = levers(n, safe, centre)
            slot = n * kd + j
            push, turn_y, turn_z = [], 0.0, 0.0
            for dx in range(2):
                wr = slot_buf[slot, dx] * fluid_buf[safe, 0, dx]
                px = wr * (slot_buf[slot, 2] - fluid_buf[safe, 1, dx])
                py = wr * (slot_buf[slot, 3 + dx] - fluid_buf[safe, 2, dx])
                pz = wr * (slot_buf[slot, 5 + dx] - fluid_buf[safe, 3, dx])
                push.append((px, py, pz))
                turn_y = turn_y - lever_x[dx] * pz
                turn_z = turn_z + lever_x[dx] * py
            px, py, pz = [u + v for u, v in zip(*push)]
            values = [
                px, py, pz,
                lever_y * pz - lever_z * py,
                turn_y + lever_z * px,
                turn_z - lever_y * px,
            ]
            for c, value in enumerate(values):
                acc[c] = acc[c] + jnp.where(second, 0.0, value)
                acc[6 + c] = acc[6 + c] + jnp.where(second, value, 0.0)
        for s in range(2):
            stack = jnp.zeros((8, 128), F32)
            for c in range(6):
                total = jnp.sum(acc[6 * s + c], axis=0, keepdims=True)
                stack = jnp.where(sub == c, total, stack)
            part_out[n, pl.ds(8 * s, 8), :] = stack
        return 0

    lax.fori_loop(0, 9, loads_of, 0)
    load_copies = []
    for a, b in OFFSETS:
        out, land = a * 3 + b, (2 - a) * 3 + (2 - b)
        copy = remote(part_out.at[out], part_in.at[land],
                      ld_send.at[out], ld_recv.at[land], a - 1, b - 1)
        copy.start()
        load_copies.append((land, copy))

    lax.fori_loop(2, nbx, collide_row, 0)

    y_copies = [
        remote(ypack.at[0], yin_ref.at[0], yr_send.at[0], yr_recv.at[0], 0, 1),
        remote(ypack.at[1], yin_ref.at[1], yr_send.at[1], yr_recv.at[1], 0, -1),
    ]
    for copy in y_copies:
        copy.start()

    total = part_out[4]
    for land, copy in load_copies:
        copy.wait_recv()
        total = total + part_in[land]
    total_ref[...] = total

    for copy in corner_copies + y_copies + x_copies:
        copy.wait_recv()
    for n, (pop, sx, sy) in enumerate(CORNERS):
        way = 0 if sy == 1 else 1
        place = (RISING if sy == 1 else FALLING).index(pop) + (0 if sx == 1 else (nx + 1) * 5)
        line = corner_in[n]
        for bz in range(nbz):
            rows = pl.ds(bz * 8, 8)
            moved = pltpu.roll(line, (place - bz) % 128, 1)
            yin_ref[way, rows, :] = jnp.where(lane == place, moved, yin_ref[way, rows, :])

    for pair in payload.values():
        for copy in pair:
            copy.wait_send()
    for copy in x_copies + corner_copies + y_copies:
        copy.wait_send()
    for _, copy in load_copies:
        copy.wait_send()


def stream_kernel(
    nx, nz, ny, post_ref, yin_ref, total_ref, out_hbm, loads_ref, planes, out_sem
):
    lane = lax.broadcasted_iota(jnp.int32, (nz, ny), 1)
    row = lax.broadcasted_iota(jnp.int32, (nz, ny), 0)

    def copy_out(x):
        return pltpu.make_async_copy(planes.at[:, x], out_hbm.at[:, x], out_sem.at[x])

    def plane_of(x, _):
        up, down = yin_ref[0], yin_ref[1]
        for pop in range(19):
            cx, cy, cz = VEL[pop]
            plane = post_ref[SLOT[pop], x + 1 - cx]
            if cy == 1:
                place = (x + 1 - cx) * 5 + RISING.index(pop)
                plane = jnp.where(
                    lane == 0, pltpu.roll(up, 128 - place, 1), pltpu.roll(plane, 1, 1)
                )
            elif cy == -1:
                place = (x + 1 - cx) * 5 + FALLING.index(pop)
                plane = jnp.where(
                    lane == 127, pltpu.roll(down, 127 - place, 1), pltpu.roll(plane, 127, 1)
                )
            if cz != 0:
                back = post_ref[SLOT[OPP[pop]], x + 1]
                plane = jnp.where(
                    row == (0 if cz == 1 else nz - 1), back,
                    pltpu.roll(plane, 1 if cz == 1 else nz - 1, 0),
                )
            planes[pop, x] = plane
        copy_out(x).start()
        return 0

    lax.fori_loop(0, nx, plane_of, 0)
    total = jnp.sum(total_ref[...], axis=1, keepdims=True) * (-1.0 / (2 * 8 * ny))
    place_s = lax.broadcasted_iota(jnp.int32, (2, 6), 0)
    place_c = lax.broadcasted_iota(jnp.int32, (2, 6), 1)
    result = jnp.zeros((2, 6), F32)
    for s in range(2):
        for c in range(6):
            value = jnp.broadcast_to(total[8 * s + c:8 * s + c + 1], (2, 6))
            result = jnp.where((place_s == s) & (place_c == c), value, result)
    loads_ref[...] = result

    def finish(x, _):
        copy_out(x).wait()
        return 0

    lax.fori_loop(0, nx, finish, 0)


def per_device(mesh_sizes, dist, fraction, send_table, recv_table, motion):
    slabs, cols = mesh_sizes
    nx, nz, ny = dist.shape[1:]
    kd = fraction.shape[4]
    slots = 9 * kd
    blocks = (nx // 2) * (nz // 8)
    hbm = pl.BlockSpec(memory_space=pltpu.HBM)
    smem = pl.BlockSpec(memory_space=pltpu.SMEM)
    vmem = pl.BlockSpec(memory_space=pltpu.VMEM)
    dma = pltpu.SemaphoreType.DMA
    post, yin, total = pl.pallas_call(
        functools.partial(step_kernel, (slabs, cols, nx, nz, ny, kd)),
        out_shape=[
            pltpu.VMEM((19, nx + 2, nz, ny), F32),
            pltpu.VMEM((2, nz, ny), F32),
            pltpu.VMEM((16, 128), F32),
        ],
        in_specs=[hbm, hbm, smem, smem, smem],
        out_specs=[vmem, vmem, vmem],
        scratch_shapes=[
            pltpu.VMEM((19, nx, nz, ny), F32),
            pltpu.VMEM((blocks, 4, 2, 8, ny), F32),
            pltpu.VMEM((9, kd, 2, 8, ny), jnp.bfloat16),
            pltpu.VMEM((9, 8, 128), F32),
            pltpu.VMEM((9, 8, 128), F32),
            pltpu.VMEM((slots + 1, N_FIELD, 8, ny), F32),
            pltpu.VMEM((2, 8, 128), jnp.int32),
            pltpu.SMEM((2, 8, 128), jnp.int32),
            pltpu.VMEM((2, nz, ny), F32),
            pltpu.VMEM((4, 8, 128), F32),
            pltpu.VMEM((4, 8, 128), F32),
            pltpu.VMEM((9, 16, 128), F32),
            pltpu.VMEM((9, 16, 128), F32),
            dma((nx // 2,)), dma((9,)), dma((9,)), dma((9,)), dma((9,)), dma((2,)),
            dma((2,)), dma((2,)), dma((2,)), dma((2,)), dma((4,)), dma((4,)),
            dma((9,)), dma((9,)),
        ],
        compiler_params=pltpu.CompilerParams(
            collective_id=0, has_side_effects=True, vmem_limit_bytes=44 << 20
        ),
        name="collide_exchange",
    )(dist, fraction, *(jnp.transpose(t, (0, 2, 3, 1, 4)) for t in (send_table, recv_table)), motion.T)
    dist_next, loads = pl.pallas_call(
        functools.partial(stream_kernel, nx, nz, ny),
        out_shape=[jax.ShapeDtypeStruct(dist.shape, F32), jax.ShapeDtypeStruct((2, 6), F32)],
        in_specs=[vmem, vmem, vmem],
        out_specs=[hbm, vmem],
        scratch_shapes=[pltpu.VMEM((19, nx, nz, ny), F32), dma((nx,))],
        compiler_params=pltpu.CompilerParams(vmem_limit_bytes=12 << 20),
        name="stream",
    )(post, yin, total)
    return (dist_next, loads.T)


def solution(mesh):
    placed = (
        P(None, "slab", None, "col"),
        P("slab", "col", None, None, None, None, None, None),
        P("slab", "col", None, None, None),
        P("slab", "col", None, None, None),
        P(None, ("slab", "col")),
    )
    return jax.shard_map(
        functools.partial(per_device, (mesh.shape["slab"], mesh.shape["col"])),
        mesh=mesh,
        in_specs=placed,
        out_specs=(P(None, "slab", None, "col"), P(None, ("slab", "col"))),
        check_vma=False,
    )
```

```python
import functools

import jax
import jax.numpy as jnp
from jax import lax
from jax.experimental import pallas as pl
from jax.experimental.pallas import tpu as pltpu
from jax.sharding import PartitionSpec as P

F32 = jnp.float32
MESH = pl.DeviceIdType.MESH
TAU = 0.9
GAP = TAU - 0.5

AXIS_PAIRS = [(1, 2, 0), (3, 4, 1), (5, 6, 2)]
PLANE_PAIRS = [(7, 8, 9, 10, 0, 1), (11, 12, 13, 14, 0, 2), (15, 16, 17, 18, 1, 2)]
VEL = [
    (0, 0, 0),
    (1, 0, 0), (-1, 0, 0), (0, 1, 0), (0, -1, 0), (0, 0, 1), (0, 0, -1),
    (1, 1, 0), (-1, -1, 0), (1, -1, 0), (-1, 1, 0),
    (1, 0, 1), (-1, 0, -1), (1, 0, -1), (-1, 0, 1),
    (0, 1, 1), (0, -1, -1), (0, 1, -1), (0, -1, 1),
]
OPP = [0, 2, 1, 4, 3, 6, 5, 8, 7, 10, 9, 12, 11, 14, 13, 16, 15, 18, 17]
KEPT = [1, 7, 9, 11, 13, 2, 8, 10, 12, 14, 0, 3, 4, 5, 6, 15, 16, 17, 18]
SLOT = {pop: place for place, pop in enumerate(KEPT)}
RISING = [3, 7, 10, 15, 17]
FALLING = [4, 8, 9, 16, 18]
CORNERS = [(7, 1, 1), (10, -1, 1), (9, 1, -1), (8, -1, -1)]
OFFSETS = [(a, b) for a in range(3) for b in range(3) if (a, b) != (1, 1)]
SEND_ORDER = [(0, 1), (2, 1), (0, 0), (2, 0), (0, 2), (2, 2), (1, 0), (1, 2)]
N_FIELD = 7


def step_kernel(
    sizes, dist_hbm, frac_hbm, send_hbm, recv_hbm, motion_hbm,
    post_ref, yin_ref, total_ref,
    cells_buf, fluid_buf, frac_in, par_out, par_in, slot_buf, table_v, table_s,
    ypack, corner_out, corner_in, part_out, part_in, send_ref, recv_ref, motion_ref,
    dist_sem, frac_send, frac_recv, par_send, par_recv, local_sem,
    xr_send, xr_recv, yr_send, yr_recv, cr_send, cr_recv, ld_send, ld_recv,
):
    slabs, cols, nx, nz, ny, kd = sizes
    nbx, nbz = nx // 2, nz // 8
    slots = 9 * kd
    me_p, me_q = lax.axis_index("slab"), lax.axis_index("col")

    def at(dp, dq):
        return (lax.rem(me_p + (dp + slabs), slabs), lax.rem(me_q + (dq + cols), cols))

    def remote(src, dst, send_sem, recv_sem, dp, dq):
        return pltpu.make_async_remote_copy(
            src_ref=src, dst_ref=dst, send_sem=send_sem, recv_sem=recv_sem,
            device_id=at(dp, dq), device_id_type=MESH,
        )

    def row_of(step):
        return lax.rem(step + (nbx - 1), nbx)

    def dist_copy(step):
        rows = pl.ds(row_of(step) * 2, 2)
        return pltpu.make_async_copy(
            dist_hbm.at[:, rows], cells_buf.at[:, rows], dist_sem.at[step]
        )

    barrier = pltpu.get_barrier_semaphore()
    for a, b in OFFSETS:
        pl.semaphore_signal(barrier, inc=1, device_id=at(a - 1, b - 1), device_id_type=MESH)

    small = [
        pltpu.make_async_copy(src, dst, local_sem.at[2 + n])
        for n, (src, dst) in enumerate(
            ((motion_hbm, motion_ref), (send_hbm, send_ref), (recv_hbm, recv_ref))
        )
    ]
    for copy in small:
        copy.start()
    for step in range(nbx):
        dist_copy(step).start()
    own_copy = pltpu.make_async_copy(frac_hbm.at[0, 0, 1, 1], frac_in.at[4], local_sem.at[0])
    own_copy.start()

    lane = lax.broadcasted_iota(jnp.int32, (8, 128), 1)
    sub = lax.broadcasted_iota(jnp.int32, (8, 128), 0)

    for copy in small:
        copy.wait()
    base = jnp.zeros((8, 128), F32)
    for s in range(2):
        for r in range(9):
            base = jnp.where(lane == 9 * s + r, motion_ref[s, r], base)
    for a in range(3):
        for b in range(3):
            row = base
            for j in range(kd):
                second = (send_ref[0, a, b, 0, j] >= nbx * nbz).astype(F32)
                row = jnp.where(lane == 18 + j, second, row)
            if (a, b) == (1, 1):
                par_in[4] = row
            else:
                par_out[a * 3 + b] = row

    pl.semaphore_wait(barrier, len(OFFSETS))
    payload = {}
    for a, b in SEND_ORDER:
        out, land = a * 3 + b, (2 - a) * 3 + (2 - b)
        payload[land] = (
            remote(par_out.at[out], par_in.at[land],
                   par_send.at[out], par_recv.at[land], a - 1, b - 1),
            remote(frac_hbm.at[0, 0, a, b], frac_in.at[land],
                   frac_send.at[out], frac_recv.at[land], a - 1, b - 1),
        )
    for part in range(2):
        for pair in payload.values():
            pair[part].start()

    first = jnp.full((8, 128), slots, jnp.int32)
    other = jnp.full((8, 128), slots, jnp.int32)
    for n in range(9):
        for j in range(kd):
            hit = lane == recv_ref[0, n // 3, n % 3, 0, j]
            free = first == slots
            other = jnp.where(hit & jnp.logical_not(free), n * kd + j, other)
            first = jnp.where(hit & free, n * kd + j, first)
    table_v[0] = first
    table_v[1] = other
    table_copy = pltpu.make_async_copy(table_v, table_s, local_sem.at[1])
    table_copy.start()
    for c in range(N_FIELD):
        slot_buf[slots, c] = jnp.zeros((8, 128), F32)
    ypack[...] = jnp.zeros_like(ypack)

    def moments_row(step, _):
        dist_copy(step).wait()
        bx = row_of(step)

        def moments_block(bz, _):
            rows = pl.ds(pl.multiple_of(bz * 8, 8), 8)
            for dx in range(2):
                x = bx * 2 + dx
                plus, minus = {}, {}
                for i in range(1, 19, 2):
                    ahead = cells_buf[i, x, rows, :]
                    back = cells_buf[i + 1, x, rows, :]
                    plus[i] = ahead + back
                    minus[i] = ahead - back
                    cells_buf[i, x, rows, :] = plus[i]
                    cells_buf[i + 1, x, rows, :] = minus[i]
                density = cells_buf[0, x, rows, :]
                for i in range(1, 19, 2):
                    density = density + plus[i]
                inverse = 1.0 / density
                mom_x = (minus[1] + (minus[7] + minus[9])) + (minus[11] + minus[13])
                mom_y = (minus[3] + (minus[7] - minus[9])) + (minus[15] + minus[17])
                mom_z = (minus[5] + (minus[11] - minus[13])) + (minus[15] - minus[17])
                block = bx * nbz + bz
                fluid_buf[block, 0, dx] = density
                fluid_buf[block, 1, dx] = mom_x * inverse
                fluid_buf[block, 2, dx] = mom_y * inverse
                fluid_buf[block, 3, dx] = mom_z * inverse
            return 0

        return lax.fori_loop(0, nbz, moments_block, 0)

    lax.fori_loop(0, nbx, moments_row, 0)

    pos_y = lane.astype(F32) + 0.5
    pos_z = sub.astype(F32) + 0.5

    def slot_place(n, j):
        block = recv_ref[0, n // 3, n % 3, 0, j]
        return block >= 0, jnp.maximum(block, 0)

    def spread(row, place):
        return jnp.broadcast_to(row[:, place:place + 1], (8, 128))

    def slot_sphere(row, j, both):
        second = spread(row, 18 + j) > 0.5
        return second, [jnp.where(second, both[9 + r], both[r]) for r in range(len(both) - 9)]

    def levers(n, safe, centre):
        a, b = n // 3, n % 3
        from_x = ((1 - a) * nx + lax.div(safe, nbz) * 2).astype(F32)
        from_y = ((1 - b) * ny).astype(F32)
        from_z = (lax.rem(safe, nbz) * 8).astype(F32)
        scale = 1.0 / ny
        lever_x = [((from_x + (dx + 0.5)) - centre[0]) * scale for dx in range(2)]
        lever_y = ((pos_y + from_y) - centre[1]) * scale
        lever_z = ((pos_z + from_z) - centre[2]) * scale
        return lever_x, lever_y, lever_z

    def rounded(value):
        return value.astype(jnp.bfloat16).astype(F32)

    def slots_of(n):
        row = par_in[n]
        both = [spread(row, r) for r in range(18)]
        for j in range(kd):
            live, safe = slot_place(n, j)
            _, prm = slot_sphere(row, j, both)
            lever_x, lever_y, lever_z = levers(n, safe, prm)
            vx, vy, vz, wx, wy, wz = prm[3:9]
            slot = n * kd + j
            slot_buf[slot, 2] = rounded(vx + (wy * lever_z - wz * lever_y))
            for dx in range(2):
                frac = frac_in[n, j, dx].astype(F32)
                weight = frac * GAP / ((1.0 - frac) + GAP)
                slot_buf[slot, dx] = jnp.where(live, weight, 0.0)
                slot_buf[slot, 3 + dx] = rounded(vy + (wz * lever_x[dx] - wx * lever_z))
                slot_buf[slot, 5 + dx] = rounded(vz + (wx * lever_y - wy * lever_x[dx]))

    def slots_group(group, _):
        start = lax.rem(3 + 6 * group, 9)
        for g, lands in enumerate(((3, 5), (0, 1, 2), (6, 7, 8))):
            @pl.when(group == g)
            def _():
                for land in lands:
                    for copy in payload[land]:
                        copy.wait_recv()
        for n in range(3):
            slots_of(start + n)
        return 0

    own_copy.wait()
    lax.fori_loop(0, 3, slots_group, 0)
    table_copy.wait()

    def collide_block(bx, bz):
        rows = pl.ds(pl.multiple_of(bz * 8, 8), 8)
        block = bx * nbz + bz
        one, two = table_s[0, 0, block], table_s[1, 0, block]
        for dx in range(2):
            x = bx * 2 + dx
            fields = []
            for slot in (one, two):
                weight = slot_buf[slot, dx]
                flow = [slot_buf[slot, 2], slot_buf[slot, 3 + dx], slot_buf[slot, 5 + dx]]
                first_m = [weight * f for f in flow]
                second_m = [
                    first_m[0] * flow[0], first_m[1] * flow[1], first_m[2] * flow[2],
                    first_m[0] * flow[1], first_m[0] * flow[2], first_m[1] * flow[2],
                ]
                fields.append([weight] + first_m + second_m)
            total = [u + v for u, v in zip(*fields)]
            solid = total[0]
            density = fluid_buf[block, 0, dx]
            vel = [fluid_buf[block, 1 + c, dx] for c in range(3)]
            relax = (1.0 - solid) * (1.0 / TAU)
            keep = 0.5 - 0.5 * relax
            keep_odd = keep - solid
            even_rho = (relax - solid) * density
            odd_rho = (relax + solid) * density
            scaled = [even_rho * v for v in vel]
            flux = [odd_rho * vel[c] + density * total[1 + c] for c in range(3)]
            t_xx = scaled[0] * vel[0] + density * total[4]
            t_yy = scaled[1] * vel[1] + density * total[5]
            t_zz = scaled[2] * vel[2] + density * total[6]
            t_xy = scaled[0] * vel[1] + density * total[7]
            t_xz = scaled[0] * vel[2] + density * total[8]
            t_yz = scaled[1] * vel[2] + density * total[9]
            rest = relax * density - 1.5 * ((t_xx + t_yy) + t_zz)
            outs = {0: (keep + keep) * cells_buf[0, x, rows, :] + (1.0 / 3.0) * rest}
            rest_axis = (1.0 / 18.0) * rest
            rest_plane = (1.0 / 36.0) * rest
            diag = [t_xx, t_yy, t_zz]
            for i, back, c in AXIS_PAIRS:
                even = keep * cells_buf[i, x, rows, :] + (rest_axis + 0.25 * diag[c])
                odd = keep_odd * cells_buf[i + 1, x, rows, :] + (1.0 / 6.0) * flux[c]
                outs[i] = even + odd
                outs[back] = even - odd
            eighth = [0.125 * d for d in diag]
            twelfth = [(1.0 / 12.0) * f for f in flux]
            cross = {(0, 1): t_xy, (0, 2): t_xz, (1, 2): t_yz}
            for i, i_back, j, j_back, c, d in PLANE_PAIRS:
                middle = rest_plane + (eighth[c] + eighth[d])
                tilt = 0.25 * cross[(c, d)]
                even = keep * cells_buf[i, x, rows, :] + (middle + tilt)
                odd = keep_odd * cells_buf[i + 1, x, rows, :] + (twelfth[c] + twelfth[d])
                outs[i] = even + odd
                outs[i_back] = even - odd
                even = keep * cells_buf[j, x, rows, :] + (middle - tilt)
                odd = keep_odd * cells_buf[j + 1, x, rows, :] + (twelfth[c] - twelfth[d])
                outs[j] = even + odd
                outs[j_back] = even - odd
            for pop in range(19):
                post_ref[SLOT[pop], x + 1, rows, :] = outs[pop]

    lane_z = lax.broadcasted_iota(jnp.int32, (nz, 128), 1)

    def pack_pair(pair):
        for way, (pops, edge) in enumerate(((RISING, 127), (FALLING, 0))):
            packed = ypack[way]
            for half in range(2):
                bx = row_of(2 * pair + half)
                for dx in range(2):
                    for m in range(5):
                        plane = post_ref[SLOT[pops[m]], bx * 2 + dx + 1]
                        place = (2 * bx + dx + 1) * 5 + m
                        turned = pltpu.roll(plane, lax.rem(place + (128 - edge), 128), 1)
                        packed = jnp.where(lane_z == place, turned, packed)
            ypack[way] = packed

    x_copies = [
        remote(post_ref.at[pl.ds(0, 5), nx], post_ref.at[pl.ds(0, 5), 0],
               xr_send.at[0], xr_recv.at[0], 1, 0),
        remote(post_ref.at[pl.ds(5, 5), 1], post_ref.at[pl.ds(5, 5), nx + 1],
               xr_send.at[1], xr_recv.at[1], -1, 0),
    ]

    def collide_pair(pair, _):
        def body(i, _):
            collide_block(row_of(2 * pair + i // nbz), lax.rem(i, nbz))

            for n in range(2):
                @pl.when((pair == 0) & (i == nbz * (n + 1) - 1))
                def _():
                    x_copies[n].start()
            return 0

        return lax.fori_loop(0, 2 * nbz, body, 0)

    collide_pair(0, 0)

    corner_copies = []
    for n, (pop, sx, sy) in enumerate(CORNERS):
        line = jnp.zeros((8, 128), F32)
        edge = 127 if sy == 1 else 0
        for bz in range(nbz):
            part = post_ref[SLOT[pop], nx if sx == 1 else 1, pl.ds(bz * 8, 8), :]
            shift = (bz - edge) % 128
            line = jnp.where(lane == bz, part if shift == 0 else pltpu.roll(part, shift, 1), line)
        corner_out[n] = line
        copy = remote(corner_out.at[n], corner_in.at[n], cr_send.at[n], cr_recv.at[n], sx, sy)
        copy.start()
        corner_copies.append(copy)

    def loads_of(n):
        row = par_in[n]
        both = [spread(row, 9 * s + r) for s in range(2) for r in range(3)]
        acc = [jnp.zeros((8, 128), F32) for _ in range(12)]
        for j in range(kd):
            _, safe = slot_place(n, j)
            second = spread(row, 18 + j) > 0.5
            centre = [jnp.where(second, both[3 + r], both[r]) for r in range(3)]
            lever_x, lever_y, lever_z = levers(n, safe, centre)
            slot = n * kd + j
            push, turn_y, turn_z = [], 0.0, 0.0
            for dx in range(2):
                wr = slot_buf[slot, dx] * fluid_buf[safe, 0, dx]
                px = wr * (slot_buf[slot, 2] - fluid_buf[safe, 1, dx])
                py = wr * (slot_buf[slot, 3 + dx] - fluid_buf[safe, 2, dx])
                pz = wr * (slot_buf[slot, 5 + dx] - fluid_buf[safe, 3, dx])
                push.append((px, py, pz))
                turn_y = turn_y - lever_x[dx] * pz
                turn_z = turn_z + lever_x[dx] * py
            px, py, pz = [u + v for u, v in zip(*push)]
            values = [
                px, py, pz,
                lever_y * pz - lever_z * py,
                turn_y + lever_z * px,
                turn_z - lever_y * px,
            ]
            for c, value in enumerate(values):
                acc[c] = acc[c] + jnp.where(second, 0.0, value)
                acc[6 + c] = acc[6 + c] + jnp.where(second, value, 0.0)
        for s in range(2):
            stack = jnp.zeros((8, 128), F32)
            for c in range(6):
                total = jnp.sum(acc[6 * s + c], axis=0, keepdims=True)
                stack = jnp.where(sub == c, total, stack)
            part_out[n, pl.ds(8 * s, 8), :] = stack

    def loads_group(group, _):
        for n in range(3):
            loads_of(3 * group + n)
        return 0

    pack_pair(0)

    def other_pair(pair, _):
        collide_pair(pair, 0)
        pack_pair(pair)
        return 0

    other_pair(1, 0)
    lax.fori_loop(0, 3, loads_group, 0)
    load_copies = []
    for a, b in SEND_ORDER:
        out, land = a * 3 + b, (2 - a) * 3 + (2 - b)
        copy = remote(part_out.at[out], part_in.at[land],
                      ld_send.at[out], ld_recv.at[land], a - 1, b - 1)
        copy.start()
        load_copies.append((land, copy))

    lax.fori_loop(2, nbx // 2, other_pair, 0)

    y_copies = [
        remote(ypack.at[0], yin_ref.at[0], yr_send.at[0], yr_recv.at[0], 0, 1),
        remote(ypack.at[1], yin_ref.at[1], yr_send.at[1], yr_recv.at[1], 0, -1),
    ]
    for copy in y_copies:
        copy.start()

    for copy in corner_copies + y_copies:
        copy.wait_recv()
    for n, (pop, sx, sy) in enumerate(CORNERS):
        way = 0 if sy == 1 else 1
        place = (RISING if sy == 1 else FALLING).index(pop) + (0 if sx == 1 else (nx + 1) * 5)
        line = corner_in[n]
        for bz in range(nbz):
            rows = pl.ds(bz * 8, 8)
            moved = pltpu.roll(line, (place - bz) % 128, 1)
            yin_ref[way, rows, :] = jnp.where(lane == place, moved, yin_ref[way, rows, :])

    total = part_out[4]
    for land, copy in load_copies:
        copy.wait_recv()
        total = total + part_in[land]
    total_ref[...] = total
    for copy in x_copies:
        copy.wait_recv()

    for pair in payload.values():
        for copy in pair:
            copy.wait_send()
    for copy in x_copies + corner_copies + y_copies:
        copy.wait_send()
    for _, copy in load_copies:
        copy.wait_send()


def stream_kernel(
    nx, nz, ny, post_ref, yin_ref, total_ref, out_hbm, loads_hbm, planes, loads_ref, out_sem
):
    lane = lax.broadcasted_iota(jnp.int32, (nz, ny), 1)
    row = lax.broadcasted_iota(jnp.int32, (nz, ny), 0)

    def copy_out(x):
        return pltpu.make_async_copy(planes.at[:, x], out_hbm.at[:, x], out_sem.at[x])

    def plane_of(x, _):
        up, down = yin_ref[0], yin_ref[1]
        for pop in range(19):
            cx, cy, cz = VEL[pop]
            plane = post_ref[SLOT[pop], x + 1 - cx]
            if cy == 1:
                place = (x + 1 - cx) * 5 + RISING.index(pop)
                plane = jnp.where(
                    lane == 0, pltpu.roll(up, 128 - place, 1), pltpu.roll(plane, 1, 1)
                )
            elif cy == -1:
                place = (x + 1 - cx) * 5 + FALLING.index(pop)
                plane = jnp.where(
                    lane == 127, pltpu.roll(down, 127 - place, 1), pltpu.roll(plane, 127, 1)
                )
            if cz != 0:
                back = post_ref[SLOT[OPP[pop]], x + 1]
                plane = jnp.where(
                    row == (0 if cz == 1 else nz - 1), back,
                    pltpu.roll(plane, 1 if cz == 1 else nz - 1, 0),
                )
            planes[pop, x] = plane
        copy_out(x).start()
        return 0

    lax.fori_loop(0, nx, plane_of, 0, unroll=4)
    total = jnp.sum(total_ref[...], axis=1, keepdims=True) * (-1.0 / (2 * 8 * ny))
    place_s = lax.broadcasted_iota(jnp.int32, (2, 6), 0)
    place_c = lax.broadcasted_iota(jnp.int32, (2, 6), 1)
    result = jnp.zeros((2, 6), F32)
    for s in range(2):
        for c in range(6):
            value = jnp.broadcast_to(total[8 * s + c:8 * s + c + 1], (2, 6))
            result = jnp.where((place_s == s) & (place_c == c), value, result)
    loads_ref[...] = result
    loads_copy = pltpu.make_async_copy(loads_ref, loads_hbm, out_sem.at[nx])
    loads_copy.start()

    def finish(x, _):
        copy_out(x).wait()
        return 0

    lax.fori_loop(0, nx, finish, 0)
    loads_copy.wait()


def per_device(mesh_sizes, dist, fraction, send_table, recv_table, motion):
    slabs, cols = mesh_sizes
    nx, nz, ny = dist.shape[1:]
    kd = fraction.shape[4]
    slots = 9 * kd
    blocks = (nx // 2) * (nz // 8)
    hbm = pl.BlockSpec(memory_space=pltpu.HBM)
    vmem = pl.BlockSpec(memory_space=pltpu.VMEM)
    dma = pltpu.SemaphoreType.DMA
    post, yin, total = pl.pallas_call(
        functools.partial(step_kernel, (slabs, cols, nx, nz, ny, kd)),
        out_shape=[
            pltpu.VMEM((19, nx + 2, nz, ny), F32),
            pltpu.VMEM((2, nz, ny), F32),
            pltpu.VMEM((16, 128), F32),
        ],
        in_specs=[hbm] * 5,
        out_specs=[vmem, vmem, vmem],
        scratch_shapes=[
            pltpu.VMEM((19, nx, nz, ny), F32),
            pltpu.VMEM((blocks, 4, 2, 8, ny), F32),
            pltpu.VMEM((9, kd, 2, 8, ny), jnp.bfloat16),
            pltpu.VMEM((9, 8, 128), F32),
            pltpu.VMEM((9, 8, 128), F32),
            pltpu.VMEM((slots + 1, N_FIELD, 8, ny), F32),
            pltpu.VMEM((2, 8, 128), jnp.int32),
            pltpu.SMEM((2, 8, 128), jnp.int32),
            pltpu.VMEM((2, nz, ny), F32),
            pltpu.VMEM((4, 8, 128), F32),
            pltpu.VMEM((4, 8, 128), F32),
            pltpu.VMEM((9, 16, 128), F32),
            pltpu.VMEM((9, 16, 128), F32),
            pltpu.SMEM((1, 3, 3, 1, kd), jnp.int32),
            pltpu.SMEM((1, 3, 3, 1, kd), jnp.int32),
            pltpu.SMEM((2, 9), F32),
            dma((nx // 2,)), dma((9,)), dma((9,)), dma((9,)), dma((9,)), dma((5,)),
            dma((2,)), dma((2,)), dma((2,)), dma((2,)), dma((4,)), dma((4,)),
            dma((9,)), dma((9,)),
        ],
        compiler_params=pltpu.CompilerParams(
            collective_id=0, has_side_effects=True, vmem_limit_bytes=44 << 20
        ),
        name="collide_exchange",
    )(dist, fraction, *(jnp.transpose(t, (0, 2, 3, 1, 4)) for t in (send_table, recv_table)), motion.T)
    dist_next, loads = pl.pallas_call(
        functools.partial(stream_kernel, nx, nz, ny),
        out_shape=[jax.ShapeDtypeStruct(dist.shape, F32), jax.ShapeDtypeStruct((2, 6), F32)],
        in_specs=[vmem, vmem, vmem],
        out_specs=[hbm, hbm],
        scratch_shapes=[
            pltpu.VMEM((19, nx, nz, ny), F32), pltpu.VMEM((2, 6), F32), dma((nx + 1,))
        ],
        compiler_params=pltpu.CompilerParams(vmem_limit_bytes=12 << 20),
        name="stream",
    )(post, yin, total)
    return (dist_next, loads.T)


def solution(mesh):
    placed = (
        P(None, "slab", None, "col"),
        P("slab", "col", None, None, None, None, None, None),
        P("slab", "col", None, None, None),
        P("slab", "col", None, None, None),
        P(None, ("slab", "col")),
    )
    return jax.shard_map(
        functools.partial(per_device, (mesh.shape["slab"], mesh.shape["col"])),
        mesh=mesh,
        in_specs=placed,
        out_specs=(P(None, "slab", None, "col"), P(None, ("slab", "col"))),
        check_vma=False,
    )
```

```python
import functools

import jax
import jax.numpy as jnp
from jax import lax
from jax.experimental import pallas as pl
from jax.experimental.pallas import tpu as pltpu
from jax.sharding import PartitionSpec as P

F32 = jnp.float32
MESH = pl.DeviceIdType.MESH
TAU = 0.9
GAP = TAU - 0.5

AXIS_PAIRS = [(1, 2, 0), (3, 4, 1), (5, 6, 2)]
PLANE_PAIRS = [(7, 8, 9, 10, 0, 1), (11, 12, 13, 14, 0, 2), (15, 16, 17, 18, 1, 2)]
VEL = [
    (0, 0, 0),
    (1, 0, 0), (-1, 0, 0), (0, 1, 0), (0, -1, 0), (0, 0, 1), (0, 0, -1),
    (1, 1, 0), (-1, -1, 0), (1, -1, 0), (-1, 1, 0),
    (1, 0, 1), (-1, 0, -1), (1, 0, -1), (-1, 0, 1),
    (0, 1, 1), (0, -1, -1), (0, 1, -1), (0, -1, 1),
]
OPP = [0, 2, 1, 4, 3, 6, 5, 8, 7, 10, 9, 12, 11, 14, 13, 16, 15, 18, 17]
KEPT = [1, 7, 9, 11, 13, 2, 8, 10, 12, 14, 0, 3, 4, 5, 6, 15, 16, 17, 18]
SLOT = {pop: place for place, pop in enumerate(KEPT)}
RISING = [3, 7, 10, 15, 17]
FALLING = [4, 8, 9, 16, 18]
CORNERS = [(7, 1, 1), (10, -1, 1), (9, 1, -1), (8, -1, -1)]
OFFSETS = [(a, b) for a in range(3) for b in range(3) if (a, b) != (1, 1)]
SEND_ORDER = [(0, 1), (2, 1), (0, 0), (2, 0), (0, 2), (2, 2), (1, 0), (1, 2)]
N_FIELD = 7


def step_kernel(
    sizes, dist_hbm, frac_hbm, send_hbm, recv_hbm, motion_hbm,
    post_ref, yin_ref, total_ref,
    cells_buf, fluid_buf, frac_in, par_out, par_in, slot_buf, table_v, table_s,
    ypack, corner_out, corner_in, part_out, part_in, send_ref, recv_ref, motion_ref,
    dist_sem, frac_send, frac_recv, par_send, par_recv, local_sem,
    xr_send, xr_recv, yr_send, yr_recv, cr_send, cr_recv, ld_send, ld_recv,
):
    slabs, cols, nx, nz, ny, kd = sizes
    nbx, nbz = nx // 2, nz // 8
    slots = 9 * kd
    me_p, me_q = lax.axis_index("slab"), lax.axis_index("col")

    def at(dp, dq):
        return (lax.rem(me_p + (dp + slabs), slabs), lax.rem(me_q + (dq + cols), cols))

    def remote(src, dst, send_sem, recv_sem, dp, dq):
        return pltpu.make_async_remote_copy(
            src_ref=src, dst_ref=dst, send_sem=send_sem, recv_sem=recv_sem,
            device_id=at(dp, dq), device_id_type=MESH,
        )

    def row_of(step):
        return lax.rem(step + (nbx - 1), nbx)

    def dist_copy(step):
        rows = pl.ds(row_of(step) * 2, 2)
        return pltpu.make_async_copy(
            dist_hbm.at[:, rows], cells_buf.at[:, rows], dist_sem.at[step]
        )

    barrier = pltpu.get_barrier_semaphore()
    for a, b in OFFSETS:
        pl.semaphore_signal(barrier, inc=1, device_id=at(a - 1, b - 1), device_id_type=MESH)

    small = [
        pltpu.make_async_copy(src, dst, local_sem.at[2 + n])
        for n, (src, dst) in enumerate(
            ((motion_hbm, motion_ref), (send_hbm, send_ref), (recv_hbm, recv_ref))
        )
    ]
    for copy in small:
        copy.start()
    for step in range(nbx):
        dist_copy(step).start()
    own_copy = pltpu.make_async_copy(frac_hbm.at[0, 0, 1, 1], frac_in.at[4], local_sem.at[0])
    own_copy.start()

    lane = lax.broadcasted_iota(jnp.int32, (8, 128), 1)
    sub = lax.broadcasted_iota(jnp.int32, (8, 128), 0)

    for copy in small:
        copy.wait()
    base = jnp.zeros((8, 128), F32)
    for s in range(2):
        for r in range(9):
            base = jnp.where(lane == 9 * s + r, motion_ref[s, r], base)
    for a in range(3):
        for b in range(3):
            row = base
            for j in range(kd):
                second = (send_ref[0, a, b, 0, j] >= nbx * nbz).astype(F32)
                row = jnp.where(lane == 18 + j, second, row)
            if (a, b) == (1, 1):
                par_in[4] = row
            else:
                par_out[a * 3 + b] = row

    pl.semaphore_wait(barrier, len(OFFSETS))
    payload = {}
    for a, b in SEND_ORDER:
        out, land = a * 3 + b, (2 - a) * 3 + (2 - b)
        payload[land] = (
            remote(par_out.at[out], par_in.at[land],
                   par_send.at[out], par_recv.at[land], a - 1, b - 1),
            remote(frac_hbm.at[0, 0, a, b], frac_in.at[land],
                   frac_send.at[out], frac_recv.at[land], a - 1, b - 1),
        )
    for part in range(2):
        for pair in payload.values():
            pair[part].start()

    first = jnp.full((8, 128), slots, jnp.int32)
    other = jnp.full((8, 128), slots, jnp.int32)
    for n in range(9):
        for j in range(kd):
            hit = lane == recv_ref[0, n // 3, n % 3, 0, j]
            free = first == slots
            other = jnp.where(hit & jnp.logical_not(free), n * kd + j, other)
            first = jnp.where(hit & free, n * kd + j, first)
    table_v[0] = first
    table_v[1] = other
    table_copy = pltpu.make_async_copy(table_v, table_s, local_sem.at[1])
    table_copy.start()
    for c in range(N_FIELD):
        slot_buf[slots, c] = jnp.zeros((8, 128), F32)
    ypack[...] = jnp.zeros_like(ypack)

    def moments_row(step, _):
        dist_copy(step).wait()
        bx = row_of(step)

        def moments_block(bz, _):
            rows = pl.ds(pl.multiple_of(bz * 8, 8), 8)
            for dx in range(2):
                x = bx * 2 + dx
                plus, minus = {}, {}
                for i in range(1, 19, 2):
                    ahead = cells_buf[i, x, rows, :]
                    back = cells_buf[i + 1, x, rows, :]
                    plus[i] = ahead + back
                    minus[i] = ahead - back
                    cells_buf[i, x, rows, :] = plus[i]
                    cells_buf[i + 1, x, rows, :] = minus[i]
                density = cells_buf[0, x, rows, :]
                for i in range(1, 19, 2):
                    density = density + plus[i]
                inverse = 1.0 / density
                mom_x = (minus[1] + (minus[7] + minus[9])) + (minus[11] + minus[13])
                mom_y = (minus[3] + (minus[7] - minus[9])) + (minus[15] + minus[17])
                mom_z = (minus[5] + (minus[11] - minus[13])) + (minus[15] - minus[17])
                block = bx * nbz + bz
                fluid_buf[block, 0, dx] = density
                fluid_buf[block, 1, dx] = mom_x * inverse
                fluid_buf[block, 2, dx] = mom_y * inverse
                fluid_buf[block, 3, dx] = mom_z * inverse
            return 0

        return lax.fori_loop(0, nbz, moments_block, 0)

    lax.fori_loop(0, nbx, moments_row, 0)

    pos_y = lane.astype(F32) + 0.5
    pos_z = sub.astype(F32) + 0.5

    def slot_place(n, j):
        block = recv_ref[0, n // 3, n % 3, 0, j]
        return block >= 0, jnp.maximum(block, 0)

    def spread(row, place):
        return jnp.broadcast_to(row[:, place:place + 1], (8, 128))

    def slot_sphere(row, j, both):
        second = spread(row, 18 + j) > 0.5
        return second, [jnp.where(second, both[9 + r], both[r]) for r in range(len(both) - 9)]

    def levers(n, safe, centre):
        a, b = n // 3, n % 3
        from_x = ((1 - a) * nx + lax.div(safe, nbz) * 2).astype(F32)
        from_y = ((1 - b) * ny).astype(F32)
        from_z = (lax.rem(safe, nbz) * 8).astype(F32)
        scale = 1.0 / ny
        lever_x = [((from_x + (dx + 0.5)) - centre[0]) * scale for dx in range(2)]
        lever_y = ((pos_y + from_y) - centre[1]) * scale
        lever_z = ((pos_z + from_z) - centre[2]) * scale
        return lever_x, lever_y, lever_z

    def rounded(value):
        return value.astype(jnp.bfloat16).astype(F32)

    def slots_of(n):
        row = par_in[n]
        both = [spread(row, r) for r in range(18)]
        for j in range(kd):
            live, safe = slot_place(n, j)
            _, prm = slot_sphere(row, j, both)
            lever_x, lever_y, lever_z = levers(n, safe, prm)
            vx, vy, vz, wx, wy, wz = prm[3:9]
            slot = n * kd + j
            slot_buf[slot, 2] = rounded(vx + (wy * lever_z - wz * lever_y))
            for dx in range(2):
                frac = frac_in[n, j, dx].astype(F32)
                weight = frac * GAP / ((1.0 - frac) + GAP)
                slot_buf[slot, dx] = jnp.where(live, weight, 0.0)
                slot_buf[slot, 3 + dx] = rounded(vy + (wz * lever_x[dx] - wx * lever_z))
                slot_buf[slot, 5 + dx] = rounded(vz + (wx * lever_y - wy * lever_x[dx]))

    def slots_group(group, _):
        start = lax.rem(3 + 6 * group, 9)
        for g, lands in enumerate(((3, 5), (0, 1, 2), (6, 7, 8))):
            @pl.when(group == g)
            def _():
                for land in lands:
                    for copy in payload[land]:
                        copy.wait_recv()
        for n in range(3):
            slots_of(start + n)
        return 0

    own_copy.wait()
    lax.fori_loop(0, 3, slots_group, 0)
    table_copy.wait()

    def collide_block(bx, bz):
        rows = pl.ds(pl.multiple_of(bz * 8, 8), 8)
        block = bx * nbz + bz
        one, two = table_s[0, 0, block], table_s[1, 0, block]
        for dx in range(2):
            x = bx * 2 + dx
            fields = []
            for slot in (one, two):
                weight = slot_buf[slot, dx]
                flow = [slot_buf[slot, 2], slot_buf[slot, 3 + dx], slot_buf[slot, 5 + dx]]
                first_m = [weight * f for f in flow]
                second_m = [
                    first_m[0] * flow[0], first_m[1] * flow[1], first_m[2] * flow[2],
                    first_m[0] * flow[1], first_m[0] * flow[2], first_m[1] * flow[2],
                ]
                fields.append([weight] + first_m + second_m)
            total = [u + v for u, v in zip(*fields)]
            solid = total[0]
            density = fluid_buf[block, 0, dx]
            vel = [fluid_buf[block, 1 + c, dx] for c in range(3)]
            relax = (1.0 - solid) * (1.0 / TAU)
            keep = 0.5 - 0.5 * relax
            keep_odd = keep - solid
            even_rho = (relax - solid) * density
            odd_rho = (relax + solid) * density
            scaled = [even_rho * v for v in vel]
            flux = [odd_rho * vel[c] + density * total[1 + c] for c in range(3)]
            t_xx = scaled[0] * vel[0] + density * total[4]
            t_yy = scaled[1] * vel[1] + density * total[5]
            t_zz = scaled[2] * vel[2] + density * total[6]
            t_xy = scaled[0] * vel[1] + density * total[7]
            t_xz = scaled[0] * vel[2] + density * total[8]
            t_yz = scaled[1] * vel[2] + density * total[9]
            rest = relax * density - 1.5 * ((t_xx + t_yy) + t_zz)
            outs = {0: (keep + keep) * cells_buf[0, x, rows, :] + (1.0 / 3.0) * rest}
            rest_axis = (1.0 / 18.0) * rest
            rest_plane = (1.0 / 36.0) * rest
            diag = [t_xx, t_yy, t_zz]
            for i, back, c in AXIS_PAIRS:
                even = keep * cells_buf[i, x, rows, :] + (rest_axis + 0.25 * diag[c])
                odd = keep_odd * cells_buf[i + 1, x, rows, :] + (1.0 / 6.0) * flux[c]
                outs[i] = even + odd
                outs[back] = even - odd
            eighth = [0.125 * d for d in diag]
            twelfth = [(1.0 / 12.0) * f for f in flux]
            cross = {(0, 1): t_xy, (0, 2): t_xz, (1, 2): t_yz}
            for i, i_back, j, j_back, c, d in PLANE_PAIRS:
                middle = rest_plane + (eighth[c] + eighth[d])
                tilt = 0.25 * cross[(c, d)]
                even = keep * cells_buf[i, x, rows, :] + (middle + tilt)
                odd = keep_odd * cells_buf[i + 1, x, rows, :] + (twelfth[c] + twelfth[d])
                outs[i] = even + odd
                outs[i_back] = even - odd
                even = keep * cells_buf[j, x, rows, :] + (middle - tilt)
                odd = keep_odd * cells_buf[j + 1, x, rows, :] + (twelfth[c] - twelfth[d])
                outs[j] = even + odd
                outs[j_back] = even - odd
            for pop in range(19):
                post_ref[SLOT[pop], x + 1, rows, :] = outs[pop]

    lane_z = lax.broadcasted_iota(jnp.int32, (nz, 128), 1)

    def pack_pair(pair):
        for way, (pops, edge) in enumerate(((RISING, 127), (FALLING, 0))):
            packed = ypack[way]
            for half in range(2):
                bx = row_of(2 * pair + half)
                for dx in range(2):
                    for m in range(5):
                        plane = post_ref[SLOT[pops[m]], bx * 2 + dx + 1]
                        place = (2 * bx + dx + 1) * 5 + m
                        turned = pltpu.roll(plane, lax.rem(place + (128 - edge), 128), 1)
                        packed = jnp.where(lane_z == place, turned, packed)
            ypack[way] = packed

    x_copies = [
        remote(post_ref.at[pl.ds(0, 5), nx], post_ref.at[pl.ds(0, 5), 0],
               xr_send.at[0], xr_recv.at[0], 1, 0),
        remote(post_ref.at[pl.ds(5, 5), 1], post_ref.at[pl.ds(5, 5), nx + 1],
               xr_send.at[1], xr_recv.at[1], -1, 0),
    ]

    def pack_tile(pair, bz):
        rows = pl.ds(pl.multiple_of(bz * 8, 8), 8)
        for way, (pops, edge) in enumerate(((RISING, 127), (FALLING, 0))):
            packed = ypack[way, rows, :]
            for half in range(2):
                bx = row_of(2 * pair + half)
                for dx in range(2):
                    for m in range(5):
                        part = post_ref[SLOT[pops[m]], bx * 2 + dx + 1, rows, :]
                        place = (2 * bx + dx + 1) * 5 + m
                        turned = pltpu.roll(part, lax.rem(place + (128 - edge), 128), 1)
                        packed = jnp.where(lane == place, turned, packed)
            ypack[way, rows, :] = packed

    def collide_two(pair, t):
        for u in range(2):
            i = 2 * t + u
            collide_block(row_of(2 * pair + i // nbz), lax.rem(i, nbz))

    def first_pair(t, _):
        collide_two(0, t)

        for n in range(2):
            @pl.when(2 * t + 2 == nbz * (n + 1))
            def _():
                x_copies[n].start()
        return 0

    lax.fori_loop(0, nbz, first_pair, 0)

    corner_copies = []
    for n, (pop, sx, sy) in enumerate(CORNERS):
        line = jnp.zeros((8, 128), F32)
        edge = 127 if sy == 1 else 0
        for bz in range(nbz):
            part = post_ref[SLOT[pop], nx if sx == 1 else 1, pl.ds(bz * 8, 8), :]
            shift = (bz - edge) % 128
            line = jnp.where(lane == bz, part if shift == 0 else pltpu.roll(part, shift, 1), line)
        corner_out[n] = line
        copy = remote(corner_out.at[n], corner_in.at[n], cr_send.at[n], cr_recv.at[n], sx, sy)
        copy.start()
        corner_copies.append(copy)

    def loads_of(n):
        row = par_in[n]
        both = [spread(row, 9 * s + r) for s in range(2) for r in range(3)]
        acc = [jnp.zeros((8, 128), F32) for _ in range(12)]
        for j in range(kd):
            _, safe = slot_place(n, j)
            second = spread(row, 18 + j) > 0.5
            centre = [jnp.where(second, both[3 + r], both[r]) for r in range(3)]
            lever_x, lever_y, lever_z = levers(n, safe, centre)
            slot = n * kd + j
            push, turn_y, turn_z = [], 0.0, 0.0
            for dx in range(2):
                wr = slot_buf[slot, dx] * fluid_buf[safe, 0, dx]
                px = wr * (slot_buf[slot, 2] - fluid_buf[safe, 1, dx])
                py = wr * (slot_buf[slot, 3 + dx] - fluid_buf[safe, 2, dx])
                pz = wr * (slot_buf[slot, 5 + dx] - fluid_buf[safe, 3, dx])
                push.append((px, py, pz))
                turn_y = turn_y - lever_x[dx] * pz
                turn_z = turn_z + lever_x[dx] * py
            px, py, pz = [u + v for u, v in zip(*push)]
            values = [
                px, py, pz,
                lever_y * pz - lever_z * py,
                turn_y + lever_z * px,
                turn_z - lever_y * px,
            ]
            for c, value in enumerate(values):
                acc[c] = acc[c] + jnp.where(second, 0.0, value)
                acc[6 + c] = acc[6 + c] + jnp.where(second, value, 0.0)
        for s in range(2):
            stack = jnp.zeros((8, 128), F32)
            for c in range(6):
                total = jnp.sum(acc[6 * s + c], axis=0, keepdims=True)
                stack = jnp.where(sub == c, total, stack)
            part_out[n, pl.ds(8 * s, 8), :] = stack

    def loads_group(group, _):
        for n in range(3):
            loads_of(3 * group + n)
        return 0

    def other_pair(pair, _):
        def body(t, _):
            pack_tile(pair - 1, t)
            collide_two(pair, t)
            return 0

        return lax.fori_loop(0, nbz, body, 0)

    other_pair(1, 0)
    lax.fori_loop(0, 3, loads_group, 0)
    load_copies = []
    for a, b in SEND_ORDER:
        out, land = a * 3 + b, (2 - a) * 3 + (2 - b)
        copy = remote(part_out.at[out], part_in.at[land],
                      ld_send.at[out], ld_recv.at[land], a - 1, b - 1)
        copy.start()
        load_copies.append((land, copy))

    lax.fori_loop(2, nbx // 2, other_pair, 0)
    pack_pair(nbx // 2 - 1)

    y_copies = [
        remote(ypack.at[0], yin_ref.at[0], yr_send.at[0], yr_recv.at[0], 0, 1),
        remote(ypack.at[1], yin_ref.at[1], yr_send.at[1], yr_recv.at[1], 0, -1),
    ]
    for copy in y_copies:
        copy.start()

    for copy in corner_copies + y_copies:
        copy.wait_recv()
    for n, (pop, sx, sy) in enumerate(CORNERS):
        way = 0 if sy == 1 else 1
        place = (RISING if sy == 1 else FALLING).index(pop) + (0 if sx == 1 else (nx + 1) * 5)
        line = corner_in[n]
        for bz in range(nbz):
            rows = pl.ds(bz * 8, 8)
            moved = pltpu.roll(line, (place - bz) % 128, 1)
            yin_ref[way, rows, :] = jnp.where(lane == place, moved, yin_ref[way, rows, :])

    total = part_out[4]
    for land, copy in load_copies:
        copy.wait_recv()
        total = total + part_in[land]
    total_ref[...] = total
    for copy in x_copies:
        copy.wait_recv()

    for pair in payload.values():
        for copy in pair:
            copy.wait_send()
    for copy in x_copies + corner_copies + y_copies:
        copy.wait_send()
    for _, copy in load_copies:
        copy.wait_send()


def stream_kernel(
    nx, nz, ny, post_ref, yin_ref, total_ref, out_hbm, loads_hbm, planes, loads_ref, out_sem
):
    lane = lax.broadcasted_iota(jnp.int32, (nz, ny), 1)
    row = lax.broadcasted_iota(jnp.int32, (nz, ny), 0)

    def copy_out(x):
        return pltpu.make_async_copy(planes.at[:, x], out_hbm.at[:, x], out_sem.at[x])

    def plane_of(x, _):
        up, down = yin_ref[0], yin_ref[1]
        for pop in range(19):
            cx, cy, cz = VEL[pop]
            plane = post_ref[SLOT[pop], x + 1 - cx]
            if cy == 1:
                place = (x + 1 - cx) * 5 + RISING.index(pop)
                plane = jnp.where(
                    lane == 0, pltpu.roll(up, 128 - place, 1), pltpu.roll(plane, 1, 1)
                )
            elif cy == -1:
                place = (x + 1 - cx) * 5 + FALLING.index(pop)
                plane = jnp.where(
                    lane == 127, pltpu.roll(down, 127 - place, 1), pltpu.roll(plane, 127, 1)
                )
            if cz != 0:
                back = post_ref[SLOT[OPP[pop]], x + 1]
                plane = jnp.where(
                    row == (0 if cz == 1 else nz - 1), back,
                    pltpu.roll(plane, 1 if cz == 1 else nz - 1, 0),
                )
            planes[pop, x] = plane
        copy_out(x).start()
        return 0

    lax.fori_loop(0, nx, plane_of, 0, unroll=4)
    total = jnp.sum(total_ref[...], axis=1, keepdims=True) * (-1.0 / (2 * 8 * ny))
    place_s = lax.broadcasted_iota(jnp.int32, (2, 6), 0)
    place_c = lax.broadcasted_iota(jnp.int32, (2, 6), 1)
    result = jnp.zeros((2, 6), F32)
    for s in range(2):
        for c in range(6):
            value = jnp.broadcast_to(total[8 * s + c:8 * s + c + 1], (2, 6))
            result = jnp.where((place_s == s) & (place_c == c), value, result)
    loads_ref[...] = result
    loads_copy = pltpu.make_async_copy(loads_ref, loads_hbm, out_sem.at[nx])
    loads_copy.start()

    def finish(x, _):
        copy_out(x).wait()
        return 0

    lax.fori_loop(0, nx, finish, 0)
    loads_copy.wait()


def per_device(mesh_sizes, dist, fraction, send_table, recv_table, motion):
    slabs, cols = mesh_sizes
    nx, nz, ny = dist.shape[1:]
    kd = fraction.shape[4]
    slots = 9 * kd
    blocks = (nx // 2) * (nz // 8)
    hbm = pl.BlockSpec(memory_space=pltpu.HBM)
    vmem = pl.BlockSpec(memory_space=pltpu.VMEM)
    dma = pltpu.SemaphoreType.DMA
    post, yin, total = pl.pallas_call(
        functools.partial(step_kernel, (slabs, cols, nx, nz, ny, kd)),
        out_shape=[
            pltpu.VMEM((19, nx + 2, nz, ny), F32),
            pltpu.VMEM((2, nz, ny), F32),
            pltpu.VMEM((16, 128), F32),
        ],
        in_specs=[hbm] * 5,
        out_specs=[vmem, vmem, vmem],
        scratch_shapes=[
            pltpu.VMEM((19, nx, nz, ny), F32),
            pltpu.VMEM((blocks, 4, 2, 8, ny), F32),
            pltpu.VMEM((9, kd, 2, 8, ny), jnp.bfloat16),
            pltpu.VMEM((9, 8, 128), F32),
            pltpu.VMEM((9, 8, 128), F32),
            pltpu.VMEM((slots + 1, N_FIELD, 8, ny), F32),
            pltpu.VMEM((2, 8, 128), jnp.int32),
            pltpu.SMEM((2, 8, 128), jnp.int32),
            pltpu.VMEM((2, nz, ny), F32),
            pltpu.VMEM((4, 8, 128), F32),
            pltpu.VMEM((4, 8, 128), F32),
            pltpu.VMEM((9, 16, 128), F32),
            pltpu.VMEM((9, 16, 128), F32),
            pltpu.SMEM((1, 3, 3, 1, kd), jnp.int32),
            pltpu.SMEM((1, 3, 3, 1, kd), jnp.int32),
            pltpu.SMEM((2, 9), F32),
            dma((nx // 2,)), dma((9,)), dma((9,)), dma((9,)), dma((9,)), dma((5,)),
            dma((2,)), dma((2,)), dma((2,)), dma((2,)), dma((4,)), dma((4,)),
            dma((9,)), dma((9,)),
        ],
        compiler_params=pltpu.CompilerParams(
            collective_id=0, has_side_effects=True, vmem_limit_bytes=44 << 20
        ),
        name="collide_exchange",
    )(dist, fraction, *(jnp.transpose(t, (0, 2, 3, 1, 4)) for t in (send_table, recv_table)), motion.T)
    dist_next, loads = pl.pallas_call(
        functools.partial(stream_kernel, nx, nz, ny),
        out_shape=[jax.ShapeDtypeStruct(dist.shape, F32), jax.ShapeDtypeStruct((2, 6), F32)],
        in_specs=[vmem, vmem, vmem],
        out_specs=[hbm, hbm],
        scratch_shapes=[
            pltpu.VMEM((19, nx, nz, ny), F32), pltpu.VMEM((2, 6), F32), dma((nx + 1,))
        ],
        compiler_params=pltpu.CompilerParams(vmem_limit_bytes=12 << 20),
        name="stream",
    )(post, yin, total)
    return (dist_next, loads.T)


def solution(mesh):
    placed = (
        P(None, "slab", None, "col"),
        P("slab", "col", None, None, None, None, None, None),
        P("slab", "col", None, None, None),
        P("slab", "col", None, None, None),
        P(None, ("slab", "col")),
    )
    return jax.shard_map(
        functools.partial(per_device, (mesh.shape["slab"], mesh.shape["col"])),
        mesh=mesh,
        in_specs=placed,
        out_specs=(P(None, "slab", None, "col"), P(None, ("slab", "col"))),
        check_vma=False,
    )
```

```python
import functools

import jax
import jax.numpy as jnp
from jax import lax
from jax.experimental import pallas as pl
from jax.experimental.pallas import tpu as pltpu
from jax.sharding import PartitionSpec as P

F32 = jnp.float32
MESH = pl.DeviceIdType.MESH
TAU = 0.9
GAP = TAU - 0.5

AXIS_PAIRS = [(1, 2, 0), (3, 4, 1), (5, 6, 2)]
PLANE_PAIRS = [(7, 8, 9, 10, 0, 1), (11, 12, 13, 14, 0, 2), (15, 16, 17, 18, 1, 2)]
VEL = [
    (0, 0, 0),
    (1, 0, 0), (-1, 0, 0), (0, 1, 0), (0, -1, 0), (0, 0, 1), (0, 0, -1),
    (1, 1, 0), (-1, -1, 0), (1, -1, 0), (-1, 1, 0),
    (1, 0, 1), (-1, 0, -1), (1, 0, -1), (-1, 0, 1),
    (0, 1, 1), (0, -1, -1), (0, 1, -1), (0, -1, 1),
]
OPP = [0, 2, 1, 4, 3, 6, 5, 8, 7, 10, 9, 12, 11, 14, 13, 16, 15, 18, 17]
KEPT = [1, 7, 9, 11, 13, 2, 8, 10, 12, 14, 0, 3, 4, 5, 6, 15, 16, 17, 18]
SLOT = {pop: place for place, pop in enumerate(KEPT)}
RISING = [3, 7, 10, 15, 17]
FALLING = [4, 8, 9, 16, 18]
CORNERS = [(7, 1, 1), (10, -1, 1), (9, 1, -1), (8, -1, -1)]
OFFSETS = [(a, b) for a in range(3) for b in range(3) if (a, b) != (1, 1)]
SEND_ORDER = [(0, 1), (2, 1), (0, 0), (2, 0), (0, 2), (2, 2), (1, 0), (1, 2)]
N_FIELD = 7
PRODUCTS = [(0, 0), (1, 1), (2, 2), (0, 1), (0, 2), (1, 2)]


def step_kernel(
    sizes, dist_hbm, frac_hbm, send_hbm, recv_hbm, motion_hbm,
    post_ref, yin_ref, total_ref,
    cells_buf, fluid_buf, frac_in, par_out, par_in, slot_buf, table_v, table_s,
    ypack, corner_out, corner_in, part_out, part_in, send_ref, recv_ref, motion_ref,
    dist_sem, frac_send, frac_recv, par_send, par_recv, local_sem,
    xr_send, xr_recv, yr_send, yr_recv, cr_send, cr_recv, ld_send, ld_recv,
):
    slabs, cols, nx, nz, ny, kd = sizes
    nbx, nbz = nx // 2, nz // 8
    slots = 9 * kd
    me_p, me_q = lax.axis_index("slab"), lax.axis_index("col")

    def at(dp, dq):
        return (lax.rem(me_p + (dp + slabs), slabs), lax.rem(me_q + (dq + cols), cols))

    def remote(src, dst, send_sem, recv_sem, dp, dq):
        return pltpu.make_async_remote_copy(
            src_ref=src, dst_ref=dst, send_sem=send_sem, recv_sem=recv_sem,
            device_id=at(dp, dq), device_id_type=MESH,
        )

    def row_of(step):
        return lax.rem(step + (nbx - 1), nbx)

    def dist_copy(step):
        rows = pl.ds(row_of(step) * 2, 2)
        return pltpu.make_async_copy(
            dist_hbm.at[:, rows], cells_buf.at[:, rows], dist_sem.at[step]
        )

    barrier = pltpu.get_barrier_semaphore()
    for a, b in OFFSETS:
        pl.semaphore_signal(barrier, inc=1, device_id=at(a - 1, b - 1), device_id_type=MESH)

    small = [
        pltpu.make_async_copy(src, dst, local_sem.at[2 + n])
        for n, (src, dst) in enumerate(
            ((motion_hbm, motion_ref), (send_hbm, send_ref), (recv_hbm, recv_ref))
        )
    ]
    for copy in small:
        copy.start()
    for step in range(nbx):
        dist_copy(step).start()
    own_copy = pltpu.make_async_copy(frac_hbm.at[0, 0, 1, 1], frac_in.at[4], local_sem.at[0])
    own_copy.start()

    lane = lax.broadcasted_iota(jnp.int32, (8, 128), 1)
    sub = lax.broadcasted_iota(jnp.int32, (8, 128), 0)

    for copy in small:
        copy.wait()
    base = jnp.zeros((8, 128), F32)
    for s in range(2):
        for r in range(9):
            base = jnp.where(lane == 9 * s + r, motion_ref[s, r], base)
    for a in range(3):
        for b in range(3):
            row = base
            for j in range(kd):
                second = (send_ref[0, a, b, 0, j] >= nbx * nbz).astype(F32)
                row = jnp.where(lane == 18 + j, second, row)
            if (a, b) == (1, 1):
                par_in[4] = row
            else:
                par_out[a * 3 + b] = row

    pl.semaphore_wait(barrier, len(OFFSETS))
    payload = {}
    for a, b in SEND_ORDER:
        out, land = a * 3 + b, (2 - a) * 3 + (2 - b)
        payload[land] = (
            remote(par_out.at[out], par_in.at[land],
                   par_send.at[out], par_recv.at[land], a - 1, b - 1),
            remote(frac_hbm.at[0, 0, a, b], frac_in.at[land],
                   frac_send.at[out], frac_recv.at[land], a - 1, b - 1),
        )
    for part in range(2):
        for pair in payload.values():
            pair[part].start()

    first = jnp.full((8, 128), slots, jnp.int32)
    other = jnp.full((8, 128), slots, jnp.int32)
    for n in range(9):
        for j in range(kd):
            hit = lane == recv_ref[0, n // 3, n % 3, 0, j]
            free = first == slots
            other = jnp.where(hit & jnp.logical_not(free), n * kd + j, other)
            first = jnp.where(hit & free, n * kd + j, first)
    table_v[0] = first
    table_v[1] = other
    table_copy = pltpu.make_async_copy(table_v, table_s, local_sem.at[1])
    table_copy.start()
    for c in range(N_FIELD):
        slot_buf[slots, c] = jnp.zeros((8, 128), F32)
    ypack[...] = jnp.zeros_like(ypack)

    def moments_row(step, _):
        dist_copy(step).wait()
        bx = row_of(step)

        def moments_block(bz, _):
            rows = pl.ds(pl.multiple_of(bz * 8, 8), 8)
            for dx in range(2):
                x = bx * 2 + dx
                plus, minus = {}, {}
                for i in range(1, 19, 2):
                    ahead = cells_buf[i, x, rows, :]
                    back = cells_buf[i + 1, x, rows, :]
                    plus[i] = ahead + back
                    minus[i] = ahead - back
                    cells_buf[i, x, rows, :] = plus[i]
                    cells_buf[i + 1, x, rows, :] = minus[i]
                density = cells_buf[0, x, rows, :]
                for i in range(1, 19, 2):
                    density = density + plus[i]
                inverse = 1.0 / density
                mom_x = (minus[1] + (minus[7] + minus[9])) + (minus[11] + minus[13])
                mom_y = (minus[3] + (minus[7] - minus[9])) + (minus[15] + minus[17])
                mom_z = (minus[5] + (minus[11] - minus[13])) + (minus[15] - minus[17])
                block = bx * nbz + bz
                mom = [mom_x, mom_y, mom_z]
                vel = [m * inverse for m in mom]
                fluid_buf[block, 0, dx] = density
                for c in range(3):
                    fluid_buf[block, 1 + c, dx] = vel[c]
                    fluid_buf[block, 4 + c, dx] = mom[c]
                for n, (c, d) in enumerate(PRODUCTS):
                    fluid_buf[block, 7 + n, dx] = mom[c] * vel[d]
            return 0

        return lax.fori_loop(0, nbz, moments_block, 0)

    lax.fori_loop(0, nbx, moments_row, 0)

    pos_y = lane.astype(F32) + 0.5
    pos_z = sub.astype(F32) + 0.5

    def slot_place(n, j):
        block = recv_ref[0, n // 3, n % 3, 0, j]
        return block >= 0, jnp.maximum(block, 0)

    def spread(row, place):
        return jnp.broadcast_to(row[:, place:place + 1], (8, 128))

    def slot_sphere(row, j, both):
        second = spread(row, 18 + j) > 0.5
        return second, [jnp.where(second, both[9 + r], both[r]) for r in range(len(both) - 9)]

    def levers(n, safe, centre):
        a, b = n // 3, n % 3
        from_x = ((1 - a) * nx + lax.div(safe, nbz) * 2).astype(F32)
        from_y = ((1 - b) * ny).astype(F32)
        from_z = (lax.rem(safe, nbz) * 8).astype(F32)
        scale = 1.0 / ny
        lever_x = [((from_x + (dx + 0.5)) - centre[0]) * scale for dx in range(2)]
        lever_y = ((pos_y + from_y) - centre[1]) * scale
        lever_z = ((pos_z + from_z) - centre[2]) * scale
        return lever_x, lever_y, lever_z

    def rounded(value):
        return value.astype(jnp.bfloat16).astype(F32)

    def slots_of(n):
        row = par_in[n]
        both = [spread(row, r) for r in range(18)]
        for j in range(kd):
            live, safe = slot_place(n, j)
            _, prm = slot_sphere(row, j, both)
            lever_x, lever_y, lever_z = levers(n, safe, prm)
            vx, vy, vz, wx, wy, wz = prm[3:9]
            slot = n * kd + j
            slot_buf[slot, 2] = rounded(vx + (wy * lever_z - wz * lever_y))
            for dx in range(2):
                frac = frac_in[n, j, dx].astype(F32)
                weight = frac * GAP / ((1.0 - frac) + GAP)
                slot_buf[slot, dx] = jnp.where(live, weight, 0.0)
                slot_buf[slot, 3 + dx] = rounded(vy + (wz * lever_x[dx] - wx * lever_z))
                slot_buf[slot, 5 + dx] = rounded(vz + (wx * lever_y - wy * lever_x[dx]))

    def slots_group(group, _):
        start = lax.rem(3 + 6 * group, 9)
        for g, lands in enumerate(((3, 5), (0, 1, 2), (6, 7, 8))):
            @pl.when(group == g)
            def _():
                for land in lands:
                    for copy in payload[land]:
                        copy.wait_recv()
        for n in range(3):
            slots_of(start + n)
        return 0

    own_copy.wait()
    lax.fori_loop(0, 3, slots_group, 0)
    table_copy.wait()

    def collide_block(bx, bz):
        rows = pl.ds(pl.multiple_of(bz * 8, 8), 8)
        block = bx * nbz + bz
        one, two = table_s[0, 0, block], table_s[1, 0, block]
        for dx in range(2):
            x = bx * 2 + dx
            density = fluid_buf[block, 0, dx]
            weights = [slot_buf[slot, dx] for slot in (one, two)]
            solid = weights[0] + weights[1]
            fields = []
            for slot, weight in zip((one, two), weights):
                flow = [slot_buf[slot, 2], slot_buf[slot, 3 + dx], slot_buf[slot, 5 + dx]]
                mass = weight * density
                first_m = [mass * f for f in flow]
                fields.append(first_m + [first_m[c] * flow[d] for c, d in PRODUCTS])
            total = [u + v for u, v in zip(*fields)]
            relax = (1.0 - solid) * (1.0 / TAU)
            keep = 0.5 - 0.5 * relax
            keep_odd = keep - solid
            even_part = relax - solid
            odd_part = relax + solid
            flux = [odd_part * fluid_buf[block, 4 + c, dx] + total[c] for c in range(3)]
            t_xx, t_yy, t_zz, t_xy, t_xz, t_yz = [
                even_part * fluid_buf[block, 7 + n, dx] + total[3 + n] for n in range(6)
            ]
            rest = relax * density - 1.5 * ((t_xx + t_yy) + t_zz)
            outs = {0: (keep + keep) * cells_buf[0, x, rows, :] + (1.0 / 3.0) * rest}
            rest_axis = (1.0 / 18.0) * rest
            rest_plane = (1.0 / 36.0) * rest
            diag = [t_xx, t_yy, t_zz]
            for i, back, c in AXIS_PAIRS:
                even = keep * cells_buf[i, x, rows, :] + (rest_axis + 0.25 * diag[c])
                odd = keep_odd * cells_buf[i + 1, x, rows, :] + (1.0 / 6.0) * flux[c]
                outs[i] = even + odd
                outs[back] = even - odd
            eighth = [0.125 * d for d in diag]
            twelfth = [(1.0 / 12.0) * f for f in flux]
            cross = {(0, 1): t_xy, (0, 2): t_xz, (1, 2): t_yz}
            for i, i_back, j, j_back, c, d in PLANE_PAIRS:
                middle = rest_plane + (eighth[c] + eighth[d])
                tilt = 0.25 * cross[(c, d)]
                even = keep * cells_buf[i, x, rows, :] + (middle + tilt)
                odd = keep_odd * cells_buf[i + 1, x, rows, :] + (twelfth[c] + twelfth[d])
                outs[i] = even + odd
                outs[i_back] = even - odd
                even = keep * cells_buf[j, x, rows, :] + (middle - tilt)
                odd = keep_odd * cells_buf[j + 1, x, rows, :] + (twelfth[c] - twelfth[d])
                outs[j] = even + odd
                outs[j_back] = even - odd
            for pop in range(19):
                post_ref[SLOT[pop], x + 1, rows, :] = outs[pop]

    lane_z = lax.broadcasted_iota(jnp.int32, (nz, 128), 1)

    def pack_pair(pair):
        for way, (pops, edge) in enumerate(((RISING, 127), (FALLING, 0))):
            packed = ypack[way]
            for half in range(2):
                bx = row_of(2 * pair + half)
                for dx in range(2):
                    for m in range(5):
                        plane = post_ref[SLOT[pops[m]], bx * 2 + dx + 1]
                        place = (2 * bx + dx + 1) * 5 + m
                        turned = pltpu.roll(plane, lax.rem(place + (128 - edge), 128), 1)
                        packed = jnp.where(lane_z == place, turned, packed)
            ypack[way] = packed

    x_copies = [
        remote(post_ref.at[pl.ds(0, 5), nx], post_ref.at[pl.ds(0, 5), 0],
               xr_send.at[0], xr_recv.at[0], 1, 0),
        remote(post_ref.at[pl.ds(5, 5), 1], post_ref.at[pl.ds(5, 5), nx + 1],
               xr_send.at[1], xr_recv.at[1], -1, 0),
    ]

    def pack_tile(pair, bz):
        rows = pl.ds(pl.multiple_of(bz * 8, 8), 8)
        for way, (pops, edge) in enumerate(((RISING, 127), (FALLING, 0))):
            packed = ypack[way, rows, :]
            for half in range(2):
                bx = row_of(2 * pair + half)
                for dx in range(2):
                    for m in range(5):
                        part = post_ref[SLOT[pops[m]], bx * 2 + dx + 1, rows, :]
                        place = (2 * bx + dx + 1) * 5 + m
                        turned = pltpu.roll(part, lax.rem(place + (128 - edge), 128), 1)
                        packed = jnp.where(lane == place, turned, packed)
            ypack[way, rows, :] = packed

    def collide_two(pair, t):
        for u in range(2):
            i = 2 * t + u
            collide_block(row_of(2 * pair + i // nbz), lax.rem(i, nbz))

    def first_pair(t, _):
        collide_two(0, t)

        for n in range(2):
            @pl.when(2 * t + 2 == nbz * (n + 1))
            def _():
                x_copies[n].start()
        return 0

    lax.fori_loop(0, nbz, first_pair, 0)

    corner_copies = []
    for n, (pop, sx, sy) in enumerate(CORNERS):
        line = jnp.zeros((8, 128), F32)
        edge = 127 if sy == 1 else 0
        for bz in range(nbz):
            part = post_ref[SLOT[pop], nx if sx == 1 else 1, pl.ds(bz * 8, 8), :]
            shift = (bz - edge) % 128
            line = jnp.where(lane == bz, part if shift == 0 else pltpu.roll(part, shift, 1), line)
        corner_out[n] = line
        copy = remote(corner_out.at[n], corner_in.at[n], cr_send.at[n], cr_recv.at[n], sx, sy)
        copy.start()
        corner_copies.append(copy)

    def loads_of(n):
        row = par_in[n]
        both = [spread(row, 9 * s + r) for s in range(2) for r in range(3)]
        acc = [jnp.zeros((8, 128), F32) for _ in range(12)]
        for j in range(kd):
            _, safe = slot_place(n, j)
            second = spread(row, 18 + j) > 0.5
            centre = [jnp.where(second, both[3 + r], both[r]) for r in range(3)]
            lever_x, lever_y, lever_z = levers(n, safe, centre)
            slot = n * kd + j
            push, turn_y, turn_z = [], 0.0, 0.0
            for dx in range(2):
                wr = slot_buf[slot, dx] * fluid_buf[safe, 0, dx]
                px = wr * (slot_buf[slot, 2] - fluid_buf[safe, 1, dx])
                py = wr * (slot_buf[slot, 3 + dx] - fluid_buf[safe, 2, dx])
                pz = wr * (slot_buf[slot, 5 + dx] - fluid_buf[safe, 3, dx])
                push.append((px, py, pz))
                turn_y = turn_y - lever_x[dx] * pz
                turn_z = turn_z + lever_x[dx] * py
            px, py, pz = [u + v for u, v in zip(*push)]
            values = [
                px, py, pz,
                lever_y * pz - lever_z * py,
                turn_y + lever_z * px,
                turn_z - lever_y * px,
            ]
            for c, value in enumerate(values):
                acc[c] = acc[c] + jnp.where(second, 0.0, value)
                acc[6 + c] = acc[6 + c] + jnp.where(second, value, 0.0)
        for s in range(2):
            stack = jnp.zeros((8, 128), F32)
            for c in range(6):
                total = jnp.sum(acc[6 * s + c], axis=0, keepdims=True)
                stack = jnp.where(sub == c, total, stack)
            part_out[n, pl.ds(8 * s, 8), :] = stack

    def loads_group(group, _):
        for n in range(3):
            loads_of(3 * group + n)
        return 0

    def other_pair(pair, _):
        def body(t, _):
            for u in range(2):
                pack_tile(pair - 1, 2 * t + u)
            for u in range(2):
                collide_two(pair, 2 * t + u)
            return 0

        return lax.fori_loop(0, nbz // 2, body, 0)

    other_pair(1, 0)
    lax.fori_loop(0, 3, loads_group, 0)
    load_copies = []
    for a, b in SEND_ORDER:
        out, land = a * 3 + b, (2 - a) * 3 + (2 - b)
        copy = remote(part_out.at[out], part_in.at[land],
                      ld_send.at[out], ld_recv.at[land], a - 1, b - 1)
        copy.start()
        load_copies.append((land, copy))
    lax.fori_loop(2, nbx // 2, other_pair, 0)
    pack_pair(nbx // 2 - 1)

    y_copies = [
        remote(ypack.at[0], yin_ref.at[0], yr_send.at[0], yr_recv.at[0], 0, 1),
        remote(ypack.at[1], yin_ref.at[1], yr_send.at[1], yr_recv.at[1], 0, -1),
    ]
    for copy in y_copies:
        copy.start()

    for copy in corner_copies + y_copies:
        copy.wait_recv()
    for n, (pop, sx, sy) in enumerate(CORNERS):
        way = 0 if sy == 1 else 1
        place = (RISING if sy == 1 else FALLING).index(pop) + (0 if sx == 1 else (nx + 1) * 5)
        line = corner_in[n]
        for bz in range(nbz):
            rows = pl.ds(bz * 8, 8)
            moved = pltpu.roll(line, (place - bz) % 128, 1)
            yin_ref[way, rows, :] = jnp.where(lane == place, moved, yin_ref[way, rows, :])

    total = part_out[4]
    for land, copy in load_copies:
        copy.wait_recv()
        total = total + part_in[land]
    total_ref[...] = total
    for copy in x_copies:
        copy.wait_recv()

    for pair in payload.values():
        for copy in pair:
            copy.wait_send()
    for copy in x_copies + corner_copies + y_copies:
        copy.wait_send()
    for _, copy in load_copies:
        copy.wait_send()


def stream_kernel(
    nx, nz, ny, post_ref, yin_ref, total_ref, out_hbm, loads_hbm, planes, loads_ref, out_sem
):
    lane = lax.broadcasted_iota(jnp.int32, (nz, ny), 1)
    row = lax.broadcasted_iota(jnp.int32, (nz, ny), 0)

    def copy_out(x):
        return pltpu.make_async_copy(planes.at[:, x], out_hbm.at[:, x], out_sem.at[x])

    def plane_of(x, _):
        up, down = yin_ref[0], yin_ref[1]
        for pop in range(19):
            cx, cy, cz = VEL[pop]
            plane = post_ref[SLOT[pop], x + 1 - cx]
            if cy == 1:
                place = (x + 1 - cx) * 5 + RISING.index(pop)
                plane = jnp.where(
                    lane == 0, pltpu.roll(up, 128 - place, 1), pltpu.roll(plane, 1, 1)
                )
            elif cy == -1:
                place = (x + 1 - cx) * 5 + FALLING.index(pop)
                plane = jnp.where(
                    lane == 127, pltpu.roll(down, 127 - place, 1), pltpu.roll(plane, 127, 1)
                )
            if cz != 0:
                back = post_ref[SLOT[OPP[pop]], x + 1]
                plane = jnp.where(
                    row == (0 if cz == 1 else nz - 1), back,
                    pltpu.roll(plane, 1 if cz == 1 else nz - 1, 0),
                )
            planes[pop, x] = plane
        copy_out(x).start()
        return 0

    lax.fori_loop(0, nx, plane_of, 0, unroll=4)
    total = jnp.sum(total_ref[...], axis=1, keepdims=True) * (-1.0 / (2 * 8 * ny))
    place_s = lax.broadcasted_iota(jnp.int32, (2, 6), 0)
    place_c = lax.broadcasted_iota(jnp.int32, (2, 6), 1)
    result = jnp.zeros((2, 6), F32)
    for s in range(2):
        for c in range(6):
            value = jnp.broadcast_to(total[8 * s + c:8 * s + c + 1], (2, 6))
            result = jnp.where((place_s == s) & (place_c == c), value, result)
    loads_ref[...] = result
    loads_copy = pltpu.make_async_copy(loads_ref, loads_hbm, out_sem.at[nx])
    loads_copy.start()

    def finish(x, _):
        copy_out(x).wait()
        return 0

    lax.fori_loop(0, nx, finish, 0)
    loads_copy.wait()


def per_device(mesh_sizes, dist, fraction, send_table, recv_table, motion):
    slabs, cols = mesh_sizes
    nx, nz, ny = dist.shape[1:]
    kd = fraction.shape[4]
    slots = 9 * kd
    blocks = (nx // 2) * (nz // 8)
    hbm = pl.BlockSpec(memory_space=pltpu.HBM)
    vmem = pl.BlockSpec(memory_space=pltpu.VMEM)
    dma = pltpu.SemaphoreType.DMA
    post, yin, total = pl.pallas_call(
        functools.partial(step_kernel, (slabs, cols, nx, nz, ny, kd)),
        out_shape=[
            pltpu.VMEM((19, nx + 2, nz, ny), F32),
            pltpu.VMEM((2, nz, ny), F32),
            pltpu.VMEM((16, 128), F32),
        ],
        in_specs=[hbm] * 5,
        out_specs=[vmem, vmem, vmem],
        scratch_shapes=[
            pltpu.VMEM((19, nx, nz, ny), F32),
            pltpu.VMEM((blocks, 13, 2, 8, ny), F32),
            pltpu.VMEM((9, kd, 2, 8, ny), jnp.bfloat16),
            pltpu.VMEM((9, 8, 128), F32),
            pltpu.VMEM((9, 8, 128), F32),
            pltpu.VMEM((slots + 1, N_FIELD, 8, ny), F32),
            pltpu.VMEM((2, 8, 128), jnp.int32),
            pltpu.SMEM((2, 8, 128), jnp.int32),
            pltpu.VMEM((2, nz, ny), F32),
            pltpu.VMEM((4, 8, 128), F32),
            pltpu.VMEM((4, 8, 128), F32),
            pltpu.VMEM((9, 16, 128), F32),
            pltpu.VMEM((9, 16, 128), F32),
            pltpu.SMEM((1, 3, 3, 1, kd), jnp.int32),
            pltpu.SMEM((1, 3, 3, 1, kd), jnp.int32),
            pltpu.SMEM((2, 9), F32),
            dma((nx // 2,)), dma((9,)), dma((9,)), dma((9,)), dma((9,)), dma((5,)),
            dma((2,)), dma((2,)), dma((2,)), dma((2,)), dma((4,)), dma((4,)),
            dma((9,)), dma((9,)),
        ],
        compiler_params=pltpu.CompilerParams(
            collective_id=0, has_side_effects=True, vmem_limit_bytes=44 << 20
        ),
        name="collide_exchange",
    )(dist, fraction, *(jnp.transpose(t, (0, 2, 3, 1, 4)) for t in (send_table, recv_table)), motion.T)
    dist_next, loads = pl.pallas_call(
        functools.partial(stream_kernel, nx, nz, ny),
        out_shape=[jax.ShapeDtypeStruct(dist.shape, F32), jax.ShapeDtypeStruct((2, 6), F32)],
        in_specs=[vmem, vmem, vmem],
        out_specs=[hbm, hbm],
        scratch_shapes=[
            pltpu.VMEM((19, nx, nz, ny), F32), pltpu.VMEM((2, 6), F32), dma((nx + 1,))
        ],
        compiler_params=pltpu.CompilerParams(vmem_limit_bytes=12 << 20),
        name="stream",
    )(post, yin, total)
    return (dist_next, loads.T)


def solution(mesh):
    placed = (
        P(None, "slab", None, "col"),
        P("slab", "col", None, None, None, None, None, None),
        P("slab", "col", None, None, None),
        P("slab", "col", None, None, None),
        P(None, ("slab", "col")),
    )
    return jax.shard_map(
        functools.partial(per_device, (mesh.shape["slab"], mesh.shape["col"])),
        mesh=mesh,
        in_specs=placed,
        out_specs=(P(None, "slab", None, "col"), P(None, ("slab", "col"))),
        check_vma=False,
    )
```

```python
import functools

import jax
import jax.numpy as jnp
from jax import lax
from jax.experimental import pallas as pl
from jax.experimental.pallas import tpu as pltpu
from jax.sharding import PartitionSpec as P

F32 = jnp.float32
MESH = pl.DeviceIdType.MESH
TAU = 0.9
GAP = TAU - 0.5

AXIS_PAIRS = [(1, 2, 0), (3, 4, 1), (5, 6, 2)]
PLANE_PAIRS = [(7, 8, 9, 10, 0, 1), (11, 12, 13, 14, 0, 2), (15, 16, 17, 18, 1, 2)]
VEL = [
    (0, 0, 0),
    (1, 0, 0), (-1, 0, 0), (0, 1, 0), (0, -1, 0), (0, 0, 1), (0, 0, -1),
    (1, 1, 0), (-1, -1, 0), (1, -1, 0), (-1, 1, 0),
    (1, 0, 1), (-1, 0, -1), (1, 0, -1), (-1, 0, 1),
    (0, 1, 1), (0, -1, -1), (0, 1, -1), (0, -1, 1),
]
OPP = [0, 2, 1, 4, 3, 6, 5, 8, 7, 10, 9, 12, 11, 14, 13, 16, 15, 18, 17]
KEPT = [1, 7, 9, 11, 13, 2, 8, 10, 12, 14, 0, 3, 4, 5, 6, 15, 16, 17, 18]
SLOT = {pop: place for place, pop in enumerate(KEPT)}
RISING = [3, 7, 10, 15, 17]
FALLING = [4, 8, 9, 16, 18]
CORNERS = [(7, 1, 1), (10, -1, 1), (9, 1, -1), (8, -1, -1)]
OFFSETS = [(a, b) for a in range(3) for b in range(3) if (a, b) != (1, 1)]
SEND_ORDER = [(0, 1), (2, 1), (0, 0), (2, 0), (0, 2), (2, 2), (1, 0), (1, 2)]
N_FIELD = 7
PRODUCTS = [(0, 0), (1, 1), (2, 2), (0, 1), (0, 2), (1, 2)]


def step_kernel(
    sizes, dist_hbm, frac_hbm, send_hbm, recv_hbm, motion_hbm,
    post_ref, yin_ref, total_ref,
    cells_buf, fluid_buf, frac_in, par_out, par_in, slot_buf, table_v, table_s,
    ypack, corner_out, corner_in, part_out, part_in, send_ref, recv_ref, motion_ref,
    dist_sem, frac_send, frac_recv, par_send, par_recv, local_sem,
    xr_send, xr_recv, yr_send, yr_recv, cr_send, cr_recv, ld_send, ld_recv,
):
    slabs, cols, nx, nz, ny, kd = sizes
    nbx, nbz = nx // 2, nz // 8
    slots = 9 * kd
    me_p, me_q = lax.axis_index("slab"), lax.axis_index("col")

    def at(dp, dq):
        return (lax.rem(me_p + (dp + slabs), slabs), lax.rem(me_q + (dq + cols), cols))

    def remote(src, dst, send_sem, recv_sem, dp, dq):
        return pltpu.make_async_remote_copy(
            src_ref=src, dst_ref=dst, send_sem=send_sem, recv_sem=recv_sem,
            device_id=at(dp, dq), device_id_type=MESH,
        )

    def row_of(step):
        return lax.rem(step + (nbx - 1), nbx)

    def dist_copy(step):
        rows = pl.ds(row_of(step) * 2, 2)
        return pltpu.make_async_copy(
            dist_hbm.at[:, rows], cells_buf.at[:, rows], dist_sem.at[step]
        )

    barrier = pltpu.get_barrier_semaphore()
    for a, b in OFFSETS:
        pl.semaphore_signal(barrier, inc=1, device_id=at(a - 1, b - 1), device_id_type=MESH)

    small = [
        pltpu.make_async_copy(src, dst, local_sem.at[2 + n])
        for n, (src, dst) in enumerate(
            ((motion_hbm, motion_ref), (send_hbm, send_ref), (recv_hbm, recv_ref))
        )
    ]
    for copy in small:
        copy.start()
    for step in range(nbx):
        dist_copy(step).start()
    own_copy = pltpu.make_async_copy(frac_hbm.at[0, 0, 1, 1], frac_in.at[4], local_sem.at[0])
    own_copy.start()

    lane = lax.broadcasted_iota(jnp.int32, (8, 128), 1)
    sub = lax.broadcasted_iota(jnp.int32, (8, 128), 0)

    for copy in small:
        copy.wait()
    base = jnp.zeros((8, 128), F32)
    for s in range(2):
        for r in range(9):
            base = jnp.where(lane == 9 * s + r, motion_ref[s, r], base)
    for a in range(3):
        for b in range(3):
            row = base
            for j in range(kd):
                second = (send_ref[0, a, b, 0, j] >= nbx * nbz).astype(F32)
                row = jnp.where(lane == 18 + j, second, row)
            if (a, b) == (1, 1):
                par_in[4] = row
            else:
                par_out[a * 3 + b] = row

    pl.semaphore_wait(barrier, len(OFFSETS))
    payload = {}
    for a, b in SEND_ORDER:
        out, land = a * 3 + b, (2 - a) * 3 + (2 - b)
        payload[land] = (
            remote(par_out.at[out], par_in.at[land],
                   par_send.at[out], par_recv.at[land], a - 1, b - 1),
            remote(frac_hbm.at[0, 0, a, b], frac_in.at[land],
                   frac_send.at[out], frac_recv.at[land], a - 1, b - 1),
        )
    for part in range(2):
        for pair in payload.values():
            pair[part].start()

    first = jnp.full((8, 128), slots, jnp.int32)
    other = jnp.full((8, 128), slots, jnp.int32)
    for n in range(9):
        for j in range(kd):
            hit = lane == recv_ref[0, n // 3, n % 3, 0, j]
            free = first == slots
            other = jnp.where(hit & jnp.logical_not(free), n * kd + j, other)
            first = jnp.where(hit & free, n * kd + j, first)
    table_v[0] = first
    table_v[1] = other
    table_copy = pltpu.make_async_copy(table_v, table_s, local_sem.at[1])
    table_copy.start()
    for c in range(N_FIELD):
        slot_buf[slots, c] = jnp.zeros((8, 128), F32)
    ypack[...] = jnp.zeros_like(ypack)

    def moments_row(step, _):
        dist_copy(step).wait()
        bx = row_of(step)

        def moments_block(bz, _):
            rows = pl.ds(pl.multiple_of(bz * 8, 8), 8)
            for dx in range(2):
                x = bx * 2 + dx
                plus, minus = {}, {}
                for i in range(1, 19, 2):
                    ahead = cells_buf[i, x, rows, :]
                    back = cells_buf[i + 1, x, rows, :]
                    plus[i] = ahead + back
                    minus[i] = ahead - back
                    cells_buf[i, x, rows, :] = plus[i]
                    cells_buf[i + 1, x, rows, :] = minus[i]
                density = cells_buf[0, x, rows, :]
                for i in range(1, 19, 2):
                    density = density + plus[i]
                inverse = 1.0 / density
                mom_x = (minus[1] + (minus[7] + minus[9])) + (minus[11] + minus[13])
                mom_y = (minus[3] + (minus[7] - minus[9])) + (minus[15] + minus[17])
                mom_z = (minus[5] + (minus[11] - minus[13])) + (minus[15] - minus[17])
                block = bx * nbz + bz
                mom = [mom_x, mom_y, mom_z]
                vel = [m * inverse for m in mom]
                fluid_buf[block, 0, dx] = density
                for c in range(3):
                    fluid_buf[block, 1 + c, dx] = vel[c]
                    fluid_buf[block, 4 + c, dx] = mom[c]
                for n, (c, d) in enumerate(PRODUCTS):
                    fluid_buf[block, 7 + n, dx] = mom[c] * vel[d]
            return 0

        return lax.fori_loop(0, nbz, moments_block, 0)

    lax.fori_loop(0, nbx, moments_row, 0)

    pos_y = lane.astype(F32) + 0.5
    pos_z = sub.astype(F32) + 0.5

    def slot_place(n, j):
        block = recv_ref[0, n // 3, n % 3, 0, j]
        return block >= 0, jnp.maximum(block, 0)

    def spread(row, place):
        return jnp.broadcast_to(row[:, place:place + 1], (8, 128))

    def slot_sphere(row, j, both):
        second = spread(row, 18 + j) > 0.5
        return second, [jnp.where(second, both[9 + r], both[r]) for r in range(len(both) - 9)]

    def levers(n, safe, centre):
        a, b = n // 3, n % 3
        from_x = ((1 - a) * nx + lax.div(safe, nbz) * 2).astype(F32)
        from_y = ((1 - b) * ny).astype(F32)
        from_z = (lax.rem(safe, nbz) * 8).astype(F32)
        scale = 1.0 / ny
        lever_x = [((from_x + (dx + 0.5)) - centre[0]) * scale for dx in range(2)]
        lever_y = ((pos_y + from_y) - centre[1]) * scale
        lever_z = ((pos_z + from_z) - centre[2]) * scale
        return lever_x, lever_y, lever_z

    def rounded(value):
        return value.astype(jnp.bfloat16).astype(F32)

    def slots_of(n):
        row = par_in[n]
        both = [spread(row, r) for r in range(18)]
        for j in range(kd):
            live, safe = slot_place(n, j)
            _, prm = slot_sphere(row, j, both)
            lever_x, lever_y, lever_z = levers(n, safe, prm)
            vx, vy, vz, wx, wy, wz = prm[3:9]
            slot = n * kd + j
            slot_buf[slot, 2] = rounded(vx + (wy * lever_z - wz * lever_y))
            for dx in range(2):
                frac = frac_in[n, j, dx].astype(F32)
                weight = frac * GAP / ((1.0 - frac) + GAP)
                slot_buf[slot, dx] = jnp.where(live, weight, 0.0)
                slot_buf[slot, 3 + dx] = rounded(vy + (wz * lever_x[dx] - wx * lever_z))
                slot_buf[slot, 5 + dx] = rounded(vz + (wx * lever_y - wy * lever_x[dx]))

    def slots_group(group, _):
        start = lax.rem(3 + 6 * group, 9)
        for g, lands in enumerate(((3, 5), (0, 1, 2), (6, 7, 8))):
            @pl.when(group == g)
            def _():
                for land in lands:
                    for copy in payload[land]:
                        copy.wait_recv()
        for n in range(3):
            slots_of(start + n)
        return 0

    own_copy.wait()
    lax.fori_loop(0, 3, slots_group, 0)
    table_copy.wait()

    def collide_block(bx, bz):
        rows = pl.ds(pl.multiple_of(bz * 8, 8), 8)
        block = bx * nbz + bz
        one, two = table_s[0, 0, block], table_s[1, 0, block]
        for dx in range(2):
            x = bx * 2 + dx
            density = fluid_buf[block, 0, dx]
            weights = [slot_buf[slot, dx] for slot in (one, two)]
            solid = weights[0] + weights[1]
            fields = []
            for slot, weight in zip((one, two), weights):
                flow = [slot_buf[slot, 2], slot_buf[slot, 3 + dx], slot_buf[slot, 5 + dx]]
                mass = weight * density
                first_m = [mass * f for f in flow]
                fields.append(first_m + [first_m[c] * flow[d] for c, d in PRODUCTS])
            total = [u + v for u, v in zip(*fields)]
            relax = (1.0 - solid) * (1.0 / TAU)
            keep = 0.5 - 0.5 * relax
            keep_odd = keep - solid
            even_part = relax - solid
            odd_part = relax + solid
            flux = [odd_part * fluid_buf[block, 4 + c, dx] + total[c] for c in range(3)]
            t_xx, t_yy, t_zz, t_xy, t_xz, t_yz = [
                even_part * fluid_buf[block, 7 + n, dx] + total[3 + n] for n in range(6)
            ]
            rest = relax * density - 1.5 * ((t_xx + t_yy) + t_zz)
            outs = {0: (keep + keep) * cells_buf[0, x, rows, :] + (1.0 / 3.0) * rest}
            rest_axis = (1.0 / 18.0) * rest
            rest_plane = (1.0 / 36.0) * rest
            diag = [t_xx, t_yy, t_zz]
            for i, back, c in AXIS_PAIRS:
                even = keep * cells_buf[i, x, rows, :] + (rest_axis + 0.25 * diag[c])
                odd = keep_odd * cells_buf[i + 1, x, rows, :] + (1.0 / 6.0) * flux[c]
                outs[i] = even + odd
                outs[back] = even - odd
            eighth = [0.125 * d for d in diag]
            twelfth = [(1.0 / 12.0) * f for f in flux]
            cross = {(0, 1): t_xy, (0, 2): t_xz, (1, 2): t_yz}
            for i, i_back, j, j_back, c, d in PLANE_PAIRS:
                middle = rest_plane + (eighth[c] + eighth[d])
                tilt = 0.25 * cross[(c, d)]
                even = keep * cells_buf[i, x, rows, :] + (middle + tilt)
                odd = keep_odd * cells_buf[i + 1, x, rows, :] + (twelfth[c] + twelfth[d])
                outs[i] = even + odd
                outs[i_back] = even - odd
                even = keep * cells_buf[j, x, rows, :] + (middle - tilt)
                odd = keep_odd * cells_buf[j + 1, x, rows, :] + (twelfth[c] - twelfth[d])
                outs[j] = even + odd
                outs[j_back] = even - odd
            for pop in range(19):
                post_ref[SLOT[pop], x + 1, rows, :] = outs[pop]

    lane_z = lax.broadcasted_iota(jnp.int32, (nz, 128), 1)

    def pack_pair(pair, ways):
        for way in ways:
            pops, edge = ((RISING, 127), (FALLING, 0))[way]
            packed = ypack[way]
            for half in range(2):
                bx = row_of(2 * pair + half)
                for dx in range(2):
                    for m in range(5):
                        plane = post_ref[SLOT[pops[m]], bx * 2 + dx + 1]
                        place = (2 * bx + dx + 1) * 5 + m
                        turned = pltpu.roll(plane, lax.rem(place + (128 - edge), 128), 1)
                        packed = jnp.where(lane_z == place, turned, packed)
            ypack[way] = packed

    x_copies = [
        remote(post_ref.at[pl.ds(0, 5), nx], post_ref.at[pl.ds(0, 5), 0],
               xr_send.at[0], xr_recv.at[0], 1, 0),
        remote(post_ref.at[pl.ds(5, 5), 1], post_ref.at[pl.ds(5, 5), nx + 1],
               xr_send.at[1], xr_recv.at[1], -1, 0),
    ]

    def pack_tile(pair, bz):
        rows = pl.ds(pl.multiple_of(bz * 8, 8), 8)
        for way, (pops, edge) in enumerate(((RISING, 127), (FALLING, 0))):
            packed = ypack[way, rows, :]
            for half in range(2):
                bx = row_of(2 * pair + half)
                for dx in range(2):
                    for m in range(5):
                        part = post_ref[SLOT[pops[m]], bx * 2 + dx + 1, rows, :]
                        place = (2 * bx + dx + 1) * 5 + m
                        turned = pltpu.roll(part, lax.rem(place + (128 - edge), 128), 1)
                        packed = jnp.where(lane == place, turned, packed)
            ypack[way, rows, :] = packed

    def collide_two(pair, t):
        for u in range(2):
            i = 2 * t + u
            collide_block(row_of(2 * pair + i // nbz), lax.rem(i, nbz))

    def first_pair(t, _):
        collide_two(0, t)

        for n in range(2):
            @pl.when(2 * t + 2 == nbz * (n + 1))
            def _():
                x_copies[n].start()
        return 0

    lax.fori_loop(0, nbz, first_pair, 0)

    corner_copies = []
    for n, (pop, sx, sy) in enumerate(CORNERS):
        line = jnp.zeros((8, 128), F32)
        edge = 127 if sy == 1 else 0
        for bz in range(nbz):
            part = post_ref[SLOT[pop], nx if sx == 1 else 1, pl.ds(bz * 8, 8), :]
            shift = (bz - edge) % 128
            line = jnp.where(lane == bz, part if shift == 0 else pltpu.roll(part, shift, 1), line)
        corner_out[n] = line
        copy = remote(corner_out.at[n], corner_in.at[n], cr_send.at[n], cr_recv.at[n], sx, sy)
        copy.start()
        corner_copies.append(copy)

    def loads_of(n):
        row = par_in[n]
        both = [spread(row, 9 * s + r) for s in range(2) for r in range(3)]
        acc = [jnp.zeros((8, 128), F32) for _ in range(12)]
        for j in range(kd):
            _, safe = slot_place(n, j)
            second = spread(row, 18 + j) > 0.5
            centre = [jnp.where(second, both[3 + r], both[r]) for r in range(3)]
            lever_x, lever_y, lever_z = levers(n, safe, centre)
            slot = n * kd + j
            push, turn_y, turn_z = [], 0.0, 0.0
            for dx in range(2):
                wr = slot_buf[slot, dx] * fluid_buf[safe, 0, dx]
                px = wr * (slot_buf[slot, 2] - fluid_buf[safe, 1, dx])
                py = wr * (slot_buf[slot, 3 + dx] - fluid_buf[safe, 2, dx])
                pz = wr * (slot_buf[slot, 5 + dx] - fluid_buf[safe, 3, dx])
                push.append((px, py, pz))
                turn_y = turn_y - lever_x[dx] * pz
                turn_z = turn_z + lever_x[dx] * py
            px, py, pz = [u + v for u, v in zip(*push)]
            values = [
                px, py, pz,
                lever_y * pz - lever_z * py,
                turn_y + lever_z * px,
                turn_z - lever_y * px,
            ]
            for c, value in enumerate(values):
                acc[c] = acc[c] + jnp.where(second, 0.0, value)
                acc[6 + c] = acc[6 + c] + jnp.where(second, value, 0.0)
        for s in range(2):
            stack = jnp.zeros((8, 128), F32)
            for c in range(6):
                total = jnp.sum(acc[6 * s + c], axis=0, keepdims=True)
                stack = jnp.where(sub == c, total, stack)
            part_out[n, pl.ds(8 * s, 8), :] = stack

    load_copies = {}
    for a, b in SEND_ORDER:
        out, land = a * 3 + b, (2 - a) * 3 + (2 - b)
        load_copies[out] = (land, remote(
            part_out.at[out], part_in.at[land], ld_send.at[out], ld_recv.at[land], a - 1, b - 1
        ))

    def loads_group(group, _):
        start = lax.rem(6 * group, 9)
        for n in range(3):
            loads_of(start + n)
        for g, outs in enumerate(((0, 1, 2), (6, 7, 8), (3, 5))):
            @pl.when(group == g)
            def _():
                for out in outs:
                    load_copies[out][1].start()
        return 0

    def other_pair(pair, _):
        def body(t, _):
            for u in range(2):
                pack_tile(pair - 1, 2 * t + u)
            for u in range(2):
                collide_two(pair, 2 * t + u)
            return 0

        return lax.fori_loop(0, nbz // 2, body, 0)

    other_pair(1, 0)
    lax.fori_loop(0, 3, loads_group, 0)
    lax.fori_loop(2, nbx // 2, other_pair, 0)

    y_copies = [
        remote(ypack.at[0], yin_ref.at[0], yr_send.at[0], yr_recv.at[0], 0, 1),
        remote(ypack.at[1], yin_ref.at[1], yr_send.at[1], yr_recv.at[1], 0, -1),
    ]
    for way in range(2):
        pack_pair(nbx // 2 - 1, (way,))
        y_copies[way].start()

    for copy in corner_copies + y_copies:
        copy.wait_recv()
    for n, (pop, sx, sy) in enumerate(CORNERS):
        way = 0 if sy == 1 else 1
        place = (RISING if sy == 1 else FALLING).index(pop) + (0 if sx == 1 else (nx + 1) * 5)
        line = corner_in[n]
        for bz in range(nbz):
            rows = pl.ds(bz * 8, 8)
            moved = pltpu.roll(line, (place - bz) % 128, 1)
            yin_ref[way, rows, :] = jnp.where(lane == place, moved, yin_ref[way, rows, :])

    total = part_out[4]
    for land, copy in load_copies.values():
        copy.wait_recv()
        total = total + part_in[land]
    total_ref[...] = total
    for copy in x_copies:
        copy.wait_recv()

    for pair in payload.values():
        for copy in pair:
            copy.wait_send()
    for copy in x_copies + corner_copies + y_copies:
        copy.wait_send()
    for _, copy in load_copies.values():
        copy.wait_send()


def stream_kernel(
    nx, nz, ny, post_ref, yin_ref, total_ref, out_hbm, loads_hbm, planes, loads_ref, out_sem
):
    lane = lax.broadcasted_iota(jnp.int32, (nz, ny), 1)
    row = lax.broadcasted_iota(jnp.int32, (nz, ny), 0)

    def copy_out(x):
        return pltpu.make_async_copy(planes.at[:, x], out_hbm.at[:, x], out_sem.at[x])

    def plane_of(x, _):
        up, down = yin_ref[0], yin_ref[1]
        for pop in range(19):
            cx, cy, cz = VEL[pop]
            plane = post_ref[SLOT[pop], x + 1 - cx]
            if cy == 1:
                place = (x + 1 - cx) * 5 + RISING.index(pop)
                plane = jnp.where(
                    lane == 0, pltpu.roll(up, 128 - place, 1), pltpu.roll(plane, 1, 1)
                )
            elif cy == -1:
                place = (x + 1 - cx) * 5 + FALLING.index(pop)
                plane = jnp.where(
                    lane == 127, pltpu.roll(down, 127 - place, 1), pltpu.roll(plane, 127, 1)
                )
            if cz != 0:
                back = post_ref[SLOT[OPP[pop]], x + 1]
                plane = jnp.where(
                    row == (0 if cz == 1 else nz - 1), back,
                    pltpu.roll(plane, 1 if cz == 1 else nz - 1, 0),
                )
            planes[pop, x] = plane
        copy_out(x).start()
        return 0

    lax.fori_loop(0, nx, plane_of, 0, unroll=4)
    total = jnp.sum(total_ref[...], axis=1, keepdims=True) * (-1.0 / (2 * 8 * ny))
    place_s = lax.broadcasted_iota(jnp.int32, (2, 6), 0)
    place_c = lax.broadcasted_iota(jnp.int32, (2, 6), 1)
    result = jnp.zeros((2, 6), F32)
    for s in range(2):
        for c in range(6):
            value = jnp.broadcast_to(total[8 * s + c:8 * s + c + 1], (2, 6))
            result = jnp.where((place_s == s) & (place_c == c), value, result)
    loads_ref[...] = result
    loads_copy = pltpu.make_async_copy(loads_ref, loads_hbm, out_sem.at[nx])
    loads_copy.start()

    def finish(x, _):
        copy_out(x).wait()
        return 0

    lax.fori_loop(0, nx, finish, 0)
    loads_copy.wait()


def per_device(mesh_sizes, dist, fraction, send_table, recv_table, motion):
    slabs, cols = mesh_sizes
    nx, nz, ny = dist.shape[1:]
    kd = fraction.shape[4]
    slots = 9 * kd
    blocks = (nx // 2) * (nz // 8)
    hbm = pl.BlockSpec(memory_space=pltpu.HBM)
    vmem = pl.BlockSpec(memory_space=pltpu.VMEM)
    dma = pltpu.SemaphoreType.DMA
    post, yin, total = pl.pallas_call(
        functools.partial(step_kernel, (slabs, cols, nx, nz, ny, kd)),
        out_shape=[
            pltpu.VMEM((19, nx + 2, nz, ny), F32),
            pltpu.VMEM((2, nz, ny), F32),
            pltpu.VMEM((16, 128), F32),
        ],
        in_specs=[hbm] * 5,
        out_specs=[vmem, vmem, vmem],
        scratch_shapes=[
            pltpu.VMEM((19, nx, nz, ny), F32),
            pltpu.VMEM((blocks, 13, 2, 8, ny), F32),
            pltpu.VMEM((9, kd, 2, 8, ny), jnp.bfloat16),
            pltpu.VMEM((9, 8, 128), F32),
            pltpu.VMEM((9, 8, 128), F32),
            pltpu.VMEM((slots + 1, N_FIELD, 8, ny), F32),
            pltpu.VMEM((2, 8, 128), jnp.int32),
            pltpu.SMEM((2, 8, 128), jnp.int32),
            pltpu.VMEM((2, nz, ny), F32),
            pltpu.VMEM((4, 8, 128), F32),
            pltpu.VMEM((4, 8, 128), F32),
            pltpu.VMEM((9, 16, 128), F32),
            pltpu.VMEM((9, 16, 128), F32),
            pltpu.SMEM((1, 3, 3, 1, kd), jnp.int32),
            pltpu.SMEM((1, 3, 3, 1, kd), jnp.int32),
            pltpu.SMEM((2, 9), F32),
            dma((nx // 2,)), dma((9,)), dma((9,)), dma((9,)), dma((9,)), dma((5,)),
            dma((2,)), dma((2,)), dma((2,)), dma((2,)), dma((4,)), dma((4,)),
            dma((9,)), dma((9,)),
        ],
        compiler_params=pltpu.CompilerParams(
            collective_id=0, has_side_effects=True, vmem_limit_bytes=44 << 20
        ),
        name="collide_exchange",
    )(dist, fraction, *(jnp.transpose(t, (0, 2, 3, 1, 4)) for t in (send_table, recv_table)), motion.T)
    dist_next, loads = pl.pallas_call(
        functools.partial(stream_kernel, nx, nz, ny),
        out_shape=[jax.ShapeDtypeStruct(dist.shape, F32), jax.ShapeDtypeStruct((2, 6), F32)],
        in_specs=[vmem, vmem, vmem],
        out_specs=[hbm, hbm],
        scratch_shapes=[
            pltpu.VMEM((19, nx, nz, ny), F32), pltpu.VMEM((2, 6), F32), dma((nx + 1,))
        ],
        compiler_params=pltpu.CompilerParams(vmem_limit_bytes=12 << 20),
        name="stream",
    )(post, yin, total)
    return (dist_next, loads.T)


def solution(mesh):
    placed = (
        P(None, "slab", None, "col"),
        P("slab", "col", None, None, None, None, None, None),
        P("slab", "col", None, None, None),
        P("slab", "col", None, None, None),
        P(None, ("slab", "col")),
    )
    return jax.shard_map(
        functools.partial(per_device, (mesh.shape["slab"], mesh.shape["col"])),
        mesh=mesh,
        in_specs=placed,
        out_specs=(P(None, "slab", None, "col"), P(None, ("slab", "col"))),
        check_vma=False,
    )
```
